256 devices in a mesh: seq: 32 (over y, z), tp: 8 (over x, core).
Axes of the slice: x: 4, y: 4, z: 8, core: 2. Of those that a mesh axis runs over, the one named last changes fastest.
Arguments:
- tokens: bfloat16 [16384, 4096], P('seq', 'tp'), may hold values from -40 to 40, as said below
- w_query: bfloat16 [4096, 2048], P(None, 'tp'), may hold values from -0.09375 to 0.09375
- w_key: bfloat16 [4096, 2048], P(None, 'tp'), may hold values from -0.09375 to 0.09375
- w_value: bfloat16 [4096, 2048], P(None, 'tp'), may hold values from -0.09375 to 0.09375
- w_gate: bfloat16 [4096, 2048], P(None, 'tp'), may hold values from -0.09375 to 0.09375
- w_out: bfloat16 [2048, 4096], P(None, 'tp'), may hold values from -0.125 to 0.125
- decay_rate: float32 [16], replicated, may hold values from 1.8310547e-05 to 0.0333333333, as said below
- state_in: float32 [16, 128, 128], P('tp'), may hold values from -192 to 192
Outputs:
- layer_out: bfloat16 [16384, 4096], P('seq', 'tp')
The draws below stay inside these ranges and needn't reach their ends.
Inputs may be any that keep to these rules, and one draw needn't show every extreme that they name: tokens have scales that vary by row and by column. `decay_rate`: each head either forgets within a few tens of positions or keeps its state over the whole slab.
All inputs are finite; a program needn't handle non-finite values.
Results may differ from the reference program's by a relative error of at most 0.0033.
Values may be sent and summed in bfloat16 or wider, within the bound.
A program may use at most 64 MiB of HBM per device.

```python
import math
import jax
import jax.numpy as jnp
from jax import lax

D = 4096
HEAD_DIM = 128
HEADS = 16
TOK_DEV = 512
ATTN_W = 2048
TOKENS = 16384
N_SEQ = 32


def draw_tokens(key, part):
    key_base, key_rows, key_cols = jax.random.split(jax.random.fold_in(key, 11), 3)
    row_scale = jnp.exp(jax.random.uniform(key_rows, (TOKENS, 1), jnp.float32, math.log(0.3), math.log(3.0)))
    col_scale = jnp.exp(jax.random.uniform(key_cols, (1, D), jnp.float32, math.log(0.3), math.log(3.0)))
    base = jnp.clip(jax.random.normal(key_base, (TOKENS, D), jnp.float32), -4.0, 4.0)
    return (base * row_scale * col_scale).astype(jnp.bfloat16)


def draw_decay_rate(key, part):
    key_kind, key_slow, key_fast = jax.random.split(jax.random.fold_in(key, 23), 3)
    picked = jax.random.uniform(key_kind, (HEADS,), jnp.float32)
    share = 0.5
    slow_rate = jnp.exp(jax.random.uniform(key_slow, (HEADS,), jnp.float32, math.log(0.3 / TOKENS), math.log(2.0 / TOKENS)))
    fast_rate = jax.random.uniform(key_fast, (HEADS,), jnp.float32, 1.0 / 50.0, 1.0 / 30.0)
    return jnp.where(picked < share, slow_rate, fast_rate).astype(jnp.float32)


def steps_of(rng, dims, cuts, low, largest):
    def one(axis_at, blocks):
        draws = jax.random.uniform(jax.random.fold_in(jax.random.fold_in(rng, 6), axis_at), (blocks,), jnp.float32, low / len(cuts), largest / len(cuts))
        return jnp.repeat(jnp.exp(draws), dims[axis_at] // blocks).reshape((-1,) + (1,) * (len(dims) - axis_at - 1))

    loudness = one(*cuts[0])
    for cut in cuts[1:]:
        loudness = loudness * one(*cut)
    return loudness


def bell_draw(key, shape, spread, bound, shards=(), dtype=jnp.bfloat16):
    values = spread * jax.random.normal(key, shape, jnp.float32)
    if shards:
        values = values * steps_of(key, shape, shards, -0.22, 0.18)
    return jnp.clip(values, -bound, bound).astype(dtype)


def setup_inputs(seed: int = 0) -> dict:
    splits = jax.random.split(jax.random.key(seed), 9)
    tokens = draw_tokens(jax.random.fold_in(splits[8], 71), 0)
    w_query = bell_draw(splits[1], (D, ATTN_W), D ** -0.5, 0.09375, ((1, 8),))
    w_key = bell_draw(splits[2], (D, ATTN_W), D ** -0.5, 0.09375, ((1, 8),))
    w_value = bell_draw(splits[3], (D, ATTN_W), D ** -0.5, 0.09375, ((1, 8),))
    w_gate = bell_draw(splits[4], (D, ATTN_W), D ** -0.5, 0.09375, ((1, 8),))
    w_out = bell_draw(splits[5], (ATTN_W, D), ATTN_W ** -0.5, 0.125, ((1, 8),))
    decay_rate = draw_decay_rate(jax.random.fold_in(splits[8], 71), 0)
    state_in = bell_draw(splits[7], (HEADS, HEAD_DIM, HEAD_DIM), 32.0, 192.0, ((0, 8),), jnp.float32)
    return {"tokens": tokens, "w_query": w_query, "w_key": w_key, "w_value": w_value, "w_gate": w_gate, "w_out": w_out, "decay_rate": decay_rate, "state_in": state_in}


def reference(tokens, w_query, w_key, w_value, w_gate, w_out, decay_rate, state_in):
    hi = lax.Precision.HIGHEST
    tok_float = tokens.astype(jnp.float32)
    inv_rms = lax.rsqrt(lax.optimization_barrier(jnp.mean(tok_float * tok_float, axis=1, keepdims=True)) + 1e-06)

    def project(weight):
        return jnp.dot(tokens, weight, preferred_element_type=jnp.float32) * inv_rms
    query = jax.nn.silu(project(w_query)).astype(jnp.bfloat16)
    key_all = jax.nn.silu(project(w_key)).astype(jnp.bfloat16)
    value = project(w_value).astype(jnp.bfloat16)
    gate = jax.nn.silu(project(w_gate))

    def split_heads(array):
        return array.reshape(N_SEQ, TOK_DEV, HEADS, HEAD_DIM).transpose(0, 2, 1, 3)
    blocks = (split_heads(query), split_heads(key_all), split_heads(value))
    positions = jnp.arange(TOK_DEV).astype(jnp.float32)
    rate_col = decay_rate[:, None]
    lower = positions[:, None] >= positions[None, :]
    gap_mask = jnp.where(lower, positions[:, None] - positions[None, :], 0.0)

    def step(carry, block):
        query_b, key_b, value_b = block
        query_f = query_b.astype(jnp.float32)
        key_f = key_b.astype(jnp.float32)
        value_f = value_b.astype(jnp.float32)
        lead_decay = jnp.exp(-rate_col * (positions[None, :] + 1.0))
        inter = jnp.einsum('hid,hde->hie', query_f * lead_decay[:, :, None], carry, precision=hi)
        scores = jnp.einsum('hid,hjd->hij', query_f, key_f)
        mask = jnp.where(lower[None], jnp.exp(-rate_col[:, :, None] * gap_mask[None]), 0.0)
        weights = (scores * mask).astype(jnp.bfloat16).astype(jnp.float32)
        intra = jnp.einsum('hij,hje->hie', weights, value_f)
        tail_decay = jnp.exp(-rate_col * (TOK_DEV - 1.0 - positions[None, :]))
        local_state = jnp.einsum('hid,hie->hde', key_f * tail_decay[:, :, None], value_f, precision=hi)
        block_decay = jnp.exp(-decay_rate * float(TOK_DEV))
        new_carry = block_decay[:, None, None] * carry + local_state
        return (new_carry, intra + inter)
    final_state, attended = lax.scan(step, state_in.astype(jnp.float32), blocks)
    norm_inv = lax.rsqrt(lax.optimization_barrier(jnp.mean(attended * attended, axis=3, keepdims=True)) + 1e-06)
    normed = (attended * norm_inv).transpose(0, 2, 1, 3).reshape(TOKENS, ATTN_W)
    hidden = (normed * gate).astype(jnp.bfloat16)
    branch = jnp.dot(hidden, w_out, preferred_element_type=jnp.float32)
    return (tok_float + branch).astype(jnp.bfloat16)
```

```python
import jax
import jax.numpy as jnp
from jax import lax
from jax.experimental import pallas as pl
from jax.experimental.pallas import tpu as pltpu
from jax.sharding import PartitionSpec as P

NX, NY, NZ = 4, 4, 8
ROWS = 512
WIDTH = 4096
HD = 128
CH = 256
BF = jnp.bfloat16
F32 = jnp.float32


def silu(z):
    return z / (1.0 + jnp.exp(-z))


def kernel(tok_in, wq, wk, wv, wg, wo, rate_ref, st_in, out_ref,
           tok, w, wov, stv, acc, sq, mask, tail, lead, kb, vb, qb, gate, intra,
           lsend, r1, rtsend, rt, ssend, srecv, hid, oacc,
           load_sem, tok_send, tok_recv, s1s, s1r, s2s, s2r, s3s, s3r, hid_send, hid_recv):
    tp = lax.axis_index("tp")
    seq = lax.axis_index("seq")
    x, core = tp // 2, tp % 2
    y, z = seq // NZ, seq % NZ
    xr, xl, xo = (x + 1) % NX, (x + 3) % NX, (x + 2) % NX
    right, left = (seq, 2 * xr + core), (seq, 2 * xl + core)
    partner = (seq, 2 * x + 1 - core)
    mine, other = core, 1 - core

    def signal(dev):
        pl.semaphore_signal(barrier, inc=1, device_id=dev, device_id_type=pl.DeviceIdType.MESH)

    def remote(src, dst, ss, rs, dev):
        return pltpu.make_async_remote_copy(
            src_ref=src, dst_ref=dst, send_sem=ss, recv_sem=rs, device_id=dev,
            device_id_type=pl.DeviceIdType.MESH)

    loads = []
    for f in range(2):
        loads.append(pltpu.make_async_copy(
            tok_in.at[:, pl.ds(f * CH, CH)], tok.at[2 * tp + f], load_sem.at[f]))
    for j, ref in enumerate((wq, wk, wv, wg)):
        loads.append(pltpu.make_async_copy(ref, w.at[j], load_sem.at[2 + j]))
    loads.append(pltpu.make_async_copy(wo, wov, load_sem.at[6]))
    loads.append(pltpu.make_async_copy(st_in, stv, load_sem.at[7]))
    for c in loads:
        c.start()

    barrier = pltpu.get_barrier_semaphore()
    signal(right)
    signal(left)
    signal(partner)
    for d in range(1, NZ):
        signal((y * NZ + (z + d) % NZ, tp))
    for d in range(1, NY):
        signal((((y + d) % NY) * NZ + z, tp))
    pl.semaphore_wait(barrier, 3 + NZ - 1 + NY - 1)

    sends = []

    def go(copy):
        copy.start()
        sends.append(copy)

    def tok_go(n, slot, dev):
        go(remote(tok.at[slot], tok.at[slot], tok_send.at[n], tok_recv.at[slot], dev))

    def tok_wait(slot):
        remote(tok.at[slot], tok.at[slot], tok_send.at[0], tok_recv.at[slot], partner).wait_recv()

    def slot(xx, cc, f):
        return (2 * xx + cc) * 2 + f

    loads[0].wait()
    tok_go(0, slot(x, mine, 0), right)
    tok_go(1, slot(x, mine, 0), partner)
    loads[1].wait()
    tok_go(2, slot(x, mine, 1), left)
    tok_go(3, slot(x, mine, 1), partner)
    tok_go(4, slot(x, mine, 1), right)
    tok_go(5, slot(x, mine, 0), left)

    rates = [rate_ref[2 * tp + h] for h in range(2)]
    pos = lax.broadcasted_iota(jnp.int32, (ROWS, HD), 0).astype(F32)
    gap = (lax.broadcasted_iota(jnp.int32, (HD, ROWS), 0) + (ROWS - HD)
           - lax.broadcasted_iota(jnp.int32, (HD, ROWS), 1))
    lower = gap >= 0
    gap_f = jnp.where(lower, gap, 0).astype(F32)
    for h in range(2):
        tail[h] = jnp.exp(-rates[h] * (ROWS - 1.0 - pos))
        lead[h] = jnp.exp(-rates[h] * (pos + 1.0))
        mask[h] = jnp.where(lower, jnp.exp(-rates[h] * gap_f), 0.0)

    def project(s1, s2, first=False):
        rows1 = pl.ds(pl.multiple_of(s1 * CH, CH), CH)
        rows2 = pl.ds(pl.multiple_of(s2 * CH, CH), CH)

        def body(j, carry):
            part = jnp.dot(tok[s1], w[j, rows1, :], preferred_element_type=F32)
            part += jnp.dot(tok[s2], w[j, rows2, :], preferred_element_type=F32)
            if first:
                acc[j] = part
            else:
                acc[j] += part
            return carry

        lax.fori_loop(0, 4, body, 0)
        a = tok[s1].astype(F32)
        b = tok[s2].astype(F32)
        a = a * a
        b = b * b
        total = (a[:, :HD] + a[:, HD:]) + (b[:, :HD] + b[:, HD:])
        if first:
            sq[...] = total
        else:
            sq[...] += total

    for c in loads[2:6]:
        c.wait()
    project(slot(x, mine, 0), slot(x, mine, 1), True)
    tok_wait(slot(x, other, 0))
    tok_wait(slot(x, other, 1))
    project(slot(x, other, 0), slot(x, other, 1))

    tok_wait(slot(xl, mine, 0))
    tok_go(6, slot(xl, mine, 0), right)
    tok_go(7, slot(xl, mine, 0), partner)
    tok_wait(slot(xr, mine, 1))
    tok_go(8, slot(xr, mine, 1), left)
    tok_go(9, slot(xr, mine, 1), partner)
    project(slot(xl, mine, 0), slot(xr, mine, 1))
    tok_wait(slot(xl, other, 0))
    tok_wait(slot(xr, other, 1))
    project(slot(xl, other, 0), slot(xr, other, 1))

    tok_wait(slot(xl, mine, 1))
    tok_go(10, slot(xl, mine, 1), partner)
    tok_wait(slot(xr, mine, 0))
    tok_go(11, slot(xr, mine, 0), partner)
    project(slot(xl, mine, 1), slot(xr, mine, 0))
    tok_wait(slot(xl, other, 1))
    tok_wait(slot(xr, other, 0))
    project(slot(xl, other, 1), slot(xr, other, 0))

    tok_wait(slot(xo, mine, 0))
    tok_go(12, slot(xo, mine, 0), partner)
    tok_wait(slot(xo, mine, 1))
    tok_go(13, slot(xo, mine, 1), partner)
    project(slot(xo, mine, 0), slot(xo, mine, 1))
    tok_wait(slot(xo, other, 0))
    tok_wait(slot(xo, other, 1))
    project(slot(xo, other, 0), slot(xo, other, 1))

    inv = lax.rsqrt(jnp.sum(sq[...], axis=1, keepdims=True) / float(WIDTH) + 1e-06)
    kb[...] = silu(acc[1] * inv).astype(BF)
    vb[...] = (acc[2] * inv).astype(BF)

    for h in range(2):
        cols = slice(h * HD, (h + 1) * HD)
        scaled = kb[:, cols].astype(F32) * tail[h]
        high = scaled.astype(BF)
        low = (scaled - high.astype(F32)).astype(BF)
        dims = (((0,), (0,)), ((), ()))
        state = lax.dot_general(high, vb[:, cols], dims, preferred_element_type=F32)
        state += lax.dot_general(low, vb[:, cols], dims, preferred_element_type=F32)
        lsend[h * 4:(h + 1) * 4] = state.astype(BF).reshape(4, 32, HD)

    far_first = (4, 3, 5, 2, 6, 1, 7)
    for n, d in enumerate(far_first):
        zz = (z + d) % NZ
        go(remote(lsend.at[zz], r1.at[z], s1s.at[n], s1r.at[z], (y * NZ + zz, tp)))
    r1[z] = lsend[z]

    qb[...] = silu(acc[0] * inv).astype(BF)
    gate[...] = silu(acc[3] * inv)

    def attend(h):
        cols = slice(h * HD, (h + 1) * HD)
        for i in range(4):
            n = (i + 1) * HD
            rows = slice(i * HD, n)
            scores = lax.dot_general(qb[rows, cols], kb[0:n, cols], (((1,), (1,)), ((), ())),
                                     preferred_element_type=F32)
            weights = (scores * mask[h, :, ROWS - n:]).astype(BF)
            intra[rows, cols] = jnp.dot(weights, vb[0:n, cols], preferred_element_type=F32)

    for d in far_first[::-1]:
        zz = (z + d) % NZ
        remote(lsend.at[zz], r1.at[zz], s1s.at[0], s1r.at[zz], partner).wait_recv()
    rate_z = rate_ref[2 * tp + z // 4]
    step = jnp.exp(jnp.full((1, HD), -rate_z * ROWS, F32))
    run = jnp.zeros((32, HD), F32)
    before = []
    for k in range(NZ):
        before.append(run)
        run = step * run + r1[k].astype(F32)
    rtsend[...] = run
    for n, d in enumerate((2, 1, 3)):
        yy = (y + d) % NY
        go(remote(rtsend, rt.at[y], s2s.at[n], s2r.at[y], (yy * NZ + z, tp)))
    rt[y] = run
    attend(0)
    for d in (1, 3, 2):
        yy = (y + d) % NY
        remote(rtsend, rt.at[yy], s2s.at[0], s2r.at[yy], partner).wait_recv()
    start = jnp.zeros((32, HD), F32)
    for k in range(NY):
        gone = jnp.maximum(y - 1 - k, 0).astype(F32) * float(NZ * ROWS)
        factor = jnp.exp(jnp.full((1, HD), -rate_z * gone, F32))
        start += jnp.where(k < y, factor, 0.0) * rt[k]
    for k in range(NZ):
        factor = jnp.exp(jnp.full((1, HD), -rate_z * float(k * ROWS), F32))
        ssend[k] = (before[k] + factor * start).astype(BF)
    for n, d in enumerate(far_first):
        zz = (z + d) % NZ
        go(remote(ssend.at[zz], srecv.at[z], s3s.at[n], s3r.at[z], (y * NZ + zz, tp)))
    srecv[z] = ssend[z]
    attend(1)
    loads[6].wait()
    loads[7].wait()
    for d in far_first[::-1]:
        zz = (z + d) % NZ
        remote(ssend.at[zz], srecv.at[zz], s3s.at[0], s3r.at[zz], partner).wait_recv()
    parts = []
    offset = (ROWS * seq).astype(F32)
    for h in range(2):
        incoming = srecv[h * 4:(h + 1) * 4].astype(F32).reshape(HD, HD)
        incoming += jnp.exp(jnp.full((1, HD), -rates[h] * offset, F32)) * stv[h]
        high = incoming.astype(BF)
        parts.append((high, (incoming - high.astype(F32)).astype(BF)))

    HALF = ROWS // 2

    def hid_go(n, sl, half, dev):
        ref = hid.at[sl, pl.ds(half * HALF, HALF)]
        go(remote(ref, ref, hid_send.at[n], hid_recv.at[2 * sl + half], dev))

    def hid_wait(sl, half):
        ref = hid.at[sl, pl.ds(half * HALF, HALF)]
        remote(ref, ref, hid_send.at[0], hid_recv.at[2 * sl + half], partner).wait_recv()

    for half in range(2):
        rows = slice(half * HALF, (half + 1) * HALF)
        for h in range(2):
            cols = slice(h * HD, (h + 1) * HD)
            q = qb[rows, cols]
            inter = jnp.dot(q, parts[h][0], preferred_element_type=F32)
            inter += jnp.dot(q, parts[h][1], preferred_element_type=F32)
            att = intra[rows, cols] + lead[h, rows, :] * inter
            norm = lax.rsqrt(jnp.mean(att * att, axis=1, keepdims=True) + 1e-06)
            hid[tp, rows, cols] = (att * norm * gate[rows, cols]).astype(BF)
        if half == 0:
            hid_go(0, tp, 0, right)
            hid_go(1, tp, 0, partner)
        else:
            hid_go(2, tp, 1, left)
            hid_go(3, tp, 1, partner)
            hid_go(4, tp, 1, right)
            hid_go(5, tp, 0, left)

    def out_part(sl, half, first=False):
        rows = slice(half * HALF, (half + 1) * HALF)
        part = jnp.dot(hid[sl, rows, :], wov[pl.ds(pl.multiple_of(sl * CH, CH), CH), :],
                       preferred_element_type=F32)
        if first:
            oacc[rows, :] = part
        else:
            oacc[rows, :] += part

    tl, tr, to = 2 * xl, 2 * xr, 2 * xo
    tpp = 2 * x + other
    out_part(tp, 0, True)
    out_part(tp, 1, True)
    hid_wait(tpp, 0)
    out_part(tpp, 0)
    hid_wait(tpp, 1)
    out_part(tpp, 1)

    hid_wait(tl + mine, 0)
    hid_go(6, tl + mine, 0, right)
    hid_go(7, tl + mine, 0, partner)
    hid_wait(tr + mine, 1)
    hid_go(8, tr + mine, 1, left)
    hid_go(9, tr + mine, 1, partner)
    out_part(tl + mine, 0)
    out_part(tr + mine, 1)
    hid_wait(tl + other, 0)
    out_part(tl + other, 0)
    hid_wait(tr + other, 1)
    out_part(tr + other, 1)

    hid_wait(tl + mine, 1)
    hid_go(10, tl + mine, 1, partner)
    hid_wait(tr + mine, 0)
    hid_go(11, tr + mine, 0, partner)
    out_part(tl + mine, 1)
    out_part(tr + mine, 0)
    hid_wait(tl + other, 1)
    out_part(tl + other, 1)
    hid_wait(tr + other, 0)
    out_part(tr + other, 0)

    hid_wait(to + mine, 0)
    hid_go(12, to + mine, 0, partner)
    hid_wait(to + mine, 1)
    hid_go(13, to + mine, 1, partner)
    out_part(to + mine, 0)
    out_part(to + mine, 1)
    hid_wait(to + other, 0)
    out_part(to + other, 0)
    hid_wait(to + other, 1)
    out_part(to + other, 1)

    for f in range(2):
        cols = slice(f * CH, (f + 1) * CH)
        out_ref[:, cols] = (tok[2 * tp + f].astype(F32) + oacc[:, cols]).astype(BF)
    for c in sends:
        c.wait_send()


def per_device(tokens, w_query, w_key, w_value, w_gate, w_out, decay_rate, state_in):
    anyspec = pl.BlockSpec(memory_space=pl.ANY)
    dma = pltpu.SemaphoreType.DMA
    return pl.pallas_call(
        kernel,
        out_shape=jax.ShapeDtypeStruct((ROWS, 512), BF),
        in_specs=[anyspec] * 6 + [pl.BlockSpec(memory_space=pltpu.SMEM), anyspec],
        out_specs=pl.BlockSpec(memory_space=pltpu.VMEM),
        scratch_shapes=[
            pltpu.VMEM((16, ROWS, CH), BF),
            pltpu.VMEM((4, WIDTH, 256), BF),
            pltpu.VMEM((2048, 512), BF),
            pltpu.VMEM((2, HD, HD), F32),
            pltpu.VMEM((4, ROWS, 256), F32),
            pltpu.VMEM((ROWS, HD), F32),
            pltpu.VMEM((2, HD, ROWS), F32),
            pltpu.VMEM((2, ROWS, HD), F32),
            pltpu.VMEM((2, ROWS, HD), F32),
            pltpu.VMEM((ROWS, 256), BF),
            pltpu.VMEM((ROWS, 256), BF),
            pltpu.VMEM((ROWS, 256), BF),
            pltpu.VMEM((ROWS, 256), F32),
            pltpu.VMEM((ROWS, 256), F32),
            pltpu.VMEM((NZ, 32, HD), BF),
            pltpu.VMEM((NZ, 32, HD), BF),
            pltpu.VMEM((32, HD), F32),
            pltpu.VMEM((NY, 32, HD), F32),
            pltpu.VMEM((NZ, 32, HD), BF),
            pltpu.VMEM((NZ, 32, HD), BF),
            pltpu.VMEM((8, ROWS, 256), BF),
            pltpu.VMEM((ROWS, 512), F32),
            dma((8,)), dma((14,)), dma((16,)), dma((7,)), dma((8,)), dma((3,)), dma((4,)),
            dma((7,)), dma((8,)), dma((14,)), dma((16,)),
        ],
        compiler_params=pltpu.CompilerParams(
            collective_id=0, has_side_effects=True, vmem_limit_bytes=56 * 1024 * 1024),
        name="lightning_layer",
    )(tokens, w_query, w_key, w_value, w_gate, w_out, decay_rate, state_in)


def solution(mesh):
    return jax.shard_map(
        per_device,
        mesh=mesh,
        in_specs=(
            P("seq", "tp"),
            P(None, "tp"),
            P(None, "tp"),
            P(None, "tp"),
            P(None, "tp"),
            P(None, "tp"),
            P(),
            P("tp", None, None),
        ),
        out_specs=P("seq", "tp"),
        check_vma=False,
    )
```

```python
import jax
import jax.numpy as jnp
from jax import lax
from jax.experimental import pallas as pl
from jax.experimental.pallas import tpu as pltpu
from jax.sharding import PartitionSpec as P

NX, NY, NZ = 4, 4, 8
ROWS = 512
WIDTH = 4096
HD = 128
CH = 256
BF = jnp.bfloat16
F32 = jnp.float32


def silu(z):
    return z / (1.0 + jnp.exp(-z))


def kernel(tok_in, wq, wk, wv, wg, wo, rate_ref, st_in, out_ref,
           tok, w, wov, stv, acc, sq, mask, tail, lead, kb, vb, qb, gate, intra,
           lsend, r1, rtsend, rt, ssend, srecv, hid, oacc,
           load_sem, tok_send, tok_recv, s1s, s1r, s2s, s2r, s3s, s3r, hid_send, hid_recv, here):
    tp = lax.axis_index("tp")
    seq = lax.axis_index("seq")
    x, core = tp // 2, tp % 2
    y, z = seq // NZ, seq % NZ
    xr, xl, xo = (x + 1) % NX, (x + 3) % NX, (x + 2) % NX
    right, left = (seq, 2 * xr + core), (seq, 2 * xl + core)
    partner = (seq, 2 * x + 1 - core)
    mine, other = core, 1 - core

    def signal(dev):
        pl.semaphore_signal(barrier, inc=1, device_id=dev, device_id_type=pl.DeviceIdType.MESH)

    def remote(src, dst, ss, rs, dev):
        return pltpu.make_async_remote_copy(
            src_ref=src, dst_ref=dst, send_sem=ss, recv_sem=rs, device_id=dev,
            device_id_type=pl.DeviceIdType.MESH)

    loads = []
    for f in range(2):
        loads.append(pltpu.make_async_copy(
            tok_in.at[:, pl.ds(f * CH, CH)], tok.at[2 * tp + f], load_sem.at[f]))
    for j, ref in enumerate((wq, wk, wv, wg)):
        loads.append(pltpu.make_async_copy(ref, w.at[j], load_sem.at[2 + j]))
    loads.append(pltpu.make_async_copy(wo, wov, load_sem.at[6]))
    loads.append(pltpu.make_async_copy(st_in, stv, load_sem.at[7]))
    for c in loads:
        c.start()

    barrier = pltpu.get_barrier_semaphore()
    z_up, z_down = (y * NZ + (z + 1) % NZ, tp), (y * NZ + (z + NZ - 1) % NZ, tp)
    y_up, y_down = (((y + 1) % NY) * NZ + z, tp), (((y + NY - 1) % NY) * NZ + z, tp)
    for dev in (right, left, partner, z_up, z_down, y_up, y_down):
        signal(dev)
    pl.semaphore_wait(barrier, 7)

    def greet(n):
        for k, dev in enumerate((z_up, z_down) + ((y_up, y_down) if n == 0 else ())):
            pl.semaphore_signal(here.at[4 * n + k], inc=1, device_id=dev,
                                device_id_type=pl.DeviceIdType.MESH)

    def greeted(n):
        for k in range(4 if n == 0 else 2):
            pl.semaphore_wait(here.at[4 * n + k], 1)

    greet(0)
    sends = []

    def go(copy):
        copy.start()
        sends.append(copy)

    HALF = ROWS // 2

    def tok_copy(n, slot, half, dev):
        ref = tok.at[slot, pl.ds(half * HALF, HALF)]
        return remote(ref, ref, tok_send.at[n], tok_recv.at[2 * slot + half], dev)

    def tok_go(slot, half, dev):
        go(tok_copy(len(sends), slot, half, dev))

    def tok_wait(slot):
        for half in range(2):
            tok_copy(0, slot, half, partner).wait_recv()

    def slot(xx, cc, f):
        return (2 * xx + cc) * 2 + f

    loads[0].wait()
    for half in range(2):
        tok_go(slot(x, mine, 0), half, right)
    loads[1].wait()
    for half in range(2):
        tok_go(slot(x, mine, 1), half, left)
    for f in range(2):
        for half in range(2):
            tok_go(slot(x, mine, f), half, partner)
    for half in range(2):
        tok_go(slot(x, mine, 1), half, right)
        tok_go(slot(x, mine, 0), half, left)

    rates = [rate_ref[2 * tp + h] for h in range(2)]
    pos = lax.broadcasted_iota(jnp.int32, (ROWS, HD), 0).astype(F32)
    gap = (lax.broadcasted_iota(jnp.int32, (HD, ROWS), 0) + (ROWS - HD)
           - lax.broadcasted_iota(jnp.int32, (HD, ROWS), 1))
    lower = gap >= 0
    gap_f = jnp.where(lower, gap, 0).astype(F32)
    for h in range(2):
        tail[h] = jnp.exp(-rates[h] * (ROWS - 1.0 - pos))
        lead[h] = jnp.exp(-rates[h] * (pos + 1.0))
        mask[h] = jnp.where(lower, jnp.exp(-rates[h] * gap_f), 0.0)

    def project(s1, s2, first=False):
        rows1 = pl.ds(pl.multiple_of(s1 * CH, CH), CH)
        rows2 = pl.ds(pl.multiple_of(s2 * CH, CH), CH)

        def body(j, carry):
            part = jnp.dot(tok[s1], w[j, rows1, :], preferred_element_type=F32)
            part += jnp.dot(tok[s2], w[j, rows2, :], preferred_element_type=F32)
            if first:
                acc[j] = part
            else:
                acc[j] += part
            return carry

        lax.fori_loop(0, 4, body, 0)
        a = tok[s1].astype(F32)
        b = tok[s2].astype(F32)
        a = a * a
        b = b * b
        total = (a[:, :HD] + a[:, HD:]) + (b[:, :HD] + b[:, HD:])
        if first:
            sq[...] = total
        else:
            sq[...] += total

    def pass_on(s_left, s_right, forward):
        for half in range(2):
            tok_copy(0, s_left, half, partner).wait_recv()
            if forward:
                tok_go(s_left, half, right)
            tok_go(s_left, half, partner)
            tok_copy(0, s_right, half, partner).wait_recv()
            if forward:
                tok_go(s_right, half, left)
            tok_go(s_right, half, partner)

    for c in loads[2:6]:
        c.wait()
    project(slot(x, mine, 0), slot(x, mine, 1), True)
    greeted(0)
    greet(1)
    tok_wait(slot(x, other, 0))
    tok_wait(slot(x, other, 1))
    project(slot(x, other, 0), slot(x, other, 1))

    pass_on(slot(xl, mine, 0), slot(xr, mine, 1), True)
    project(slot(xl, mine, 0), slot(xr, mine, 1))
    greeted(1)
    greet(2)
    tok_wait(slot(xl, other, 0))
    tok_wait(slot(xr, other, 1))
    project(slot(xl, other, 0), slot(xr, other, 1))

    pass_on(slot(xl, mine, 1), slot(xr, mine, 0), False)
    project(slot(xl, mine, 1), slot(xr, mine, 0))
    tok_wait(slot(xl, other, 1))
    tok_wait(slot(xr, other, 0))
    project(slot(xl, other, 1), slot(xr, other, 0))

    pass_on(slot(xo, mine, 0), slot(xo, mine, 1), False)
    project(slot(xo, mine, 0), slot(xo, mine, 1))
    tok_wait(slot(xo, other, 0))
    tok_wait(slot(xo, other, 1))
    project(slot(xo, other, 0), slot(xo, other, 1))
    greeted(2)

    inv = lax.rsqrt(jnp.sum(sq[...], axis=1, keepdims=True) / float(WIDTH) + 1e-06)
    kb[...] = silu(acc[1] * inv).astype(BF)
    vb[...] = (acc[2] * inv).astype(BF)

    for h in range(2):
        cols = slice(h * HD, (h + 1) * HD)
        scaled = kb[:, cols].astype(F32) * tail[h]
        high = scaled.astype(BF)
        low = (scaled - high.astype(F32)).astype(BF)
        dims = (((0,), (0,)), ((), ()))
        state = lax.dot_general(high, vb[:, cols], dims, preferred_element_type=F32)
        state += lax.dot_general(low, vb[:, cols], dims, preferred_element_type=F32)
        lsend[h * 4:(h + 1) * 4] = state.astype(BF).reshape(4, 32, HD)

    far_first = (4, 3, 5, 2, 6, 1, 7)
    for n, d in enumerate(far_first):
        zz = (z + d) % NZ
        go(remote(lsend.at[zz], r1.at[z], s1s.at[n], s1r.at[z], (y * NZ + zz, tp)))
    r1[z] = lsend[z]

    qb[...] = silu(acc[0] * inv).astype(BF)
    gate[...] = silu(acc[3] * inv)

    def attend(h):
        cols = slice(h * HD, (h + 1) * HD)
        for i in range(4):
            n = (i + 1) * HD
            rows = slice(i * HD, n)
            scores = lax.dot_general(qb[rows, cols], kb[0:n, cols], (((1,), (1,)), ((), ())),
                                     preferred_element_type=F32)
            weights = (scores * mask[h, :, ROWS - n:]).astype(BF)
            intra[rows, cols] = jnp.dot(weights, vb[0:n, cols], preferred_element_type=F32)

    for d in far_first[::-1]:
        zz = (z + d) % NZ
        remote(lsend.at[zz], r1.at[zz], s1s.at[0], s1r.at[zz], partner).wait_recv()
    rate_z = rate_ref[2 * tp + z // 4]
    step = jnp.exp(jnp.full((1, HD), -rate_z * ROWS, F32))
    run = jnp.zeros((32, HD), F32)
    before = []
    for k in range(NZ):
        before.append(run)
        run = step * run + r1[k].astype(F32)
    rtsend[...] = run
    for n, d in enumerate((2, 1, 3)):
        yy = (y + d) % NY
        go(remote(rtsend, rt.at[y], s2s.at[n], s2r.at[y], (yy * NZ + z, tp)))
    rt[y] = run
    attend(0)
    for d in (1, 3, 2):
        yy = (y + d) % NY
        remote(rtsend, rt.at[yy], s2s.at[0], s2r.at[yy], partner).wait_recv()
    start = jnp.zeros((32, HD), F32)
    for k in range(NY):
        gone = jnp.maximum(y - 1 - k, 0).astype(F32) * float(NZ * ROWS)
        factor = jnp.exp(jnp.full((1, HD), -rate_z * gone, F32))
        start += jnp.where(k < y, factor, 0.0) * rt[k]
    for k in range(NZ):
        factor = jnp.exp(jnp.full((1, HD), -rate_z * float(k * ROWS), F32))
        ssend[k] = (before[k] + factor * start).astype(BF)
    for n, d in enumerate(far_first):
        zz = (z + d) % NZ
        go(remote(ssend.at[zz], srecv.at[z], s3s.at[n], s3r.at[z], (y * NZ + zz, tp)))
    srecv[z] = ssend[z]
    attend(1)
    loads[6].wait()
    loads[7].wait()
    for d in far_first[::-1]:
        zz = (z + d) % NZ
        remote(ssend.at[zz], srecv.at[zz], s3s.at[0], s3r.at[zz], partner).wait_recv()
    parts = []
    offset = (ROWS * seq).astype(F32)
    for h in range(2):
        incoming = srecv[h * 4:(h + 1) * 4].astype(F32).reshape(HD, HD)
        incoming += jnp.exp(jnp.full((1, HD), -rates[h] * offset, F32)) * stv[h]
        high = incoming.astype(BF)
        parts.append((high, (incoming - high.astype(F32)).astype(BF)))

    def hid_go(n, sl, half, dev):
        ref = hid.at[sl, pl.ds(half * HALF, HALF)]
        go(remote(ref, ref, hid_send.at[n], hid_recv.at[2 * sl + half], dev))

    def hid_wait(sl, half):
        ref = hid.at[sl, pl.ds(half * HALF, HALF)]
        remote(ref, ref, hid_send.at[0], hid_recv.at[2 * sl + half], partner).wait_recv()

    for half in range(2):
        rows = slice(half * HALF, (half + 1) * HALF)
        for h in range(2):
            cols = slice(h * HD, (h + 1) * HD)
            q = qb[rows, cols]
            inter = jnp.dot(q, parts[h][0], preferred_element_type=F32)
            inter += jnp.dot(q, parts[h][1], preferred_element_type=F32)
            att = intra[rows, cols] + lead[h, rows, :] * inter
            norm = lax.rsqrt(jnp.mean(att * att, axis=1, keepdims=True) + 1e-06)
            hid[tp, rows, cols] = (att * norm * gate[rows, cols]).astype(BF)
        if half == 0:
            hid_go(0, tp, 0, right)
            hid_go(1, tp, 0, partner)
        else:
            hid_go(2, tp, 1, left)
            hid_go(3, tp, 1, partner)
            hid_go(4, tp, 1, right)
            hid_go(5, tp, 0, left)

    def out_part(sl, half, first=False):
        rows = slice(half * HALF, (half + 1) * HALF)
        part = jnp.dot(hid[sl, rows, :], wov[pl.ds(pl.multiple_of(sl * CH, CH), CH), :],
                       preferred_element_type=F32)
        if first:
            oacc[rows, :] = part
        else:
            oacc[rows, :] += part

    tl, tr, to = 2 * xl, 2 * xr, 2 * xo
    tpp = 2 * x + other
    out_part(tp, 0, True)
    out_part(tp, 1, True)
    hid_wait(tpp, 0)
    out_part(tpp, 0)
    hid_wait(tpp, 1)
    out_part(tpp, 1)

    hid_wait(tl + mine, 0)
    hid_go(6, tl + mine, 0, right)
    hid_go(7, tl + mine, 0, partner)
    hid_wait(tr + mine, 1)
    hid_go(8, tr + mine, 1, left)
    hid_go(9, tr + mine, 1, partner)
    out_part(tl + mine, 0)
    out_part(tr + mine, 1)
    hid_wait(tl + other, 0)
    out_part(tl + other, 0)
    hid_wait(tr + other, 1)
    out_part(tr + other, 1)

    hid_wait(tl + mine, 1)
    hid_go(10, tl + mine, 1, partner)
    hid_wait(tr + mine, 0)
    hid_go(11, tr + mine, 0, partner)
    out_part(tl + mine, 1)
    out_part(tr + mine, 0)
    hid_wait(tl + other, 1)
    out_part(tl + other, 1)
    hid_wait(tr + other, 0)
    out_part(tr + other, 0)

    hid_wait(to + mine, 0)
    hid_go(12, to + mine, 0, partner)
    hid_wait(to + mine, 1)
    hid_go(13, to + mine, 1, partner)
    out_part(to + mine, 0)
    out_part(to + mine, 1)
    hid_wait(to + other, 0)
    out_part(to + other, 0)
    hid_wait(to + other, 1)
    out_part(to + other, 1)

    for f in range(2):
        cols = slice(f * CH, (f + 1) * CH)
        out_ref[:, cols] = (tok[2 * tp + f].astype(F32) + oacc[:, cols]).astype(BF)
    for c in sends:
        c.wait_send()


def per_device(tokens, w_query, w_key, w_value, w_gate, w_out, decay_rate, state_in):
    anyspec = pl.BlockSpec(memory_space=pl.ANY)
    dma = pltpu.SemaphoreType.DMA
    return pl.pallas_call(
        kernel,
        out_shape=jax.ShapeDtypeStruct((ROWS, 512), BF),
        in_specs=[anyspec] * 6 + [pl.BlockSpec(memory_space=pltpu.SMEM), anyspec],
        out_specs=pl.BlockSpec(memory_space=pltpu.VMEM),
        scratch_shapes=[
            pltpu.VMEM((16, ROWS, CH), BF),
            pltpu.VMEM((4, WIDTH, 256), BF),
            pltpu.VMEM((2048, 512), BF),
            pltpu.VMEM((2, HD, HD), F32),
            pltpu.VMEM((4, ROWS, 256), F32),
            pltpu.VMEM((ROWS, HD), F32),
            pltpu.VMEM((2, HD, ROWS), F32),
            pltpu.VMEM((2, ROWS, HD), F32),
            pltpu.VMEM((2, ROWS, HD), F32),
            pltpu.VMEM((ROWS, 256), BF),
            pltpu.VMEM((ROWS, 256), BF),
            pltpu.VMEM((ROWS, 256), BF),
            pltpu.VMEM((ROWS, 256), F32),
            pltpu.VMEM((ROWS, 256), F32),
            pltpu.VMEM((NZ, 32, HD), BF),
            pltpu.VMEM((NZ, 32, HD), BF),
            pltpu.VMEM((32, HD), F32),
            pltpu.VMEM((NY, 32, HD), F32),
            pltpu.VMEM((NZ, 32, HD), BF),
            pltpu.VMEM((NZ, 32, HD), BF),
            pltpu.VMEM((8, ROWS, 256), BF),
            pltpu.VMEM((ROWS, 512), F32),
            dma((8,)), dma((28,)), dma((32,)), dma((7,)), dma((8,)), dma((3,)), dma((4,)),
            dma((7,)), dma((8,)), dma((14,)), dma((16,)),
            pltpu.SemaphoreType.REGULAR((10,)),
        ],
        compiler_params=pltpu.CompilerParams(
            collective_id=0, has_side_effects=True, vmem_limit_bytes=56 * 1024 * 1024),
        name="lightning_layer",
    )(tokens, w_query, w_key, w_value, w_gate, w_out, decay_rate, state_in)


def solution(mesh):
    return jax.shard_map(
        per_device,
        mesh=mesh,
        in_specs=(
            P("seq", "tp"),
            P(None, "tp"),
            P(None, "tp"),
            P(None, "tp"),
            P(None, "tp"),
            P(None, "tp"),
            P(),
            P("tp", None, None),
        ),
        out_specs=P("seq", "tp"),
        check_vma=False,
    )
```

```python
import jax
import jax.numpy as jnp
from jax import lax
from jax.experimental import pallas as pl
from jax.experimental.pallas import tpu as pltpu
from jax.sharding import PartitionSpec as P

NX, NY, NZ = 4, 4, 8
ROWS = 512
WIDTH = 4096
HD = 128
CH = 256
BF = jnp.bfloat16
F32 = jnp.float32


def silu(z):
    return z / (1.0 + jnp.exp(-z))


def kernel(tok_in, wq, wk, wv, wg, wo, rate_ref, st_in, out_ref,
           tok, w, wov, stv, acc, sq, mask, tail, lead, kb, vb, qb, gate, intra,
           lsend, r1, rtsend, rt, ssend, srecv, hid, oacc,
           load_sem, tok_send, tok_recv, s1s, s1r, s2s, s2r, s3s, s3r, hid_send, hid_recv, here):
    tp = lax.axis_index("tp")
    seq = lax.axis_index("seq")
    x, core = tp // 2, tp % 2
    y, z = seq // NZ, seq % NZ
    xr, xl, xo = (x + 1) % NX, (x + 3) % NX, (x + 2) % NX
    right, left = (seq, 2 * xr + core), (seq, 2 * xl + core)
    partner = (seq, 2 * x + 1 - core)
    mine, other = core, 1 - core

    def signal(dev):
        pl.semaphore_signal(barrier, inc=1, device_id=dev, device_id_type=pl.DeviceIdType.MESH)

    def remote(src, dst, ss, rs, dev):
        return pltpu.make_async_remote_copy(
            src_ref=src, dst_ref=dst, send_sem=ss, recv_sem=rs, device_id=dev,
            device_id_type=pl.DeviceIdType.MESH)

    loads = []
    for f in range(2):
        loads.append(pltpu.make_async_copy(
            tok_in.at[:, pl.ds(f * CH, CH)], tok.at[2 * tp + f], load_sem.at[f]))
    for j, ref in enumerate((wq, wk, wv, wg)):
        loads.append(pltpu.make_async_copy(ref, w.at[j], load_sem.at[2 + j]))
    loads.append(pltpu.make_async_copy(wo, wov, load_sem.at[6]))
    loads.append(pltpu.make_async_copy(st_in, stv, load_sem.at[7]))
    for c in loads:
        c.start()

    barrier = pltpu.get_barrier_semaphore()
    z_up, z_down = (y * NZ + (z + 1) % NZ, tp), (y * NZ + (z + NZ - 1) % NZ, tp)
    y_up, y_down = (((y + 1) % NY) * NZ + z, tp), (((y + NY - 1) % NY) * NZ + z, tp)
    for dev in (right, left, partner, z_up, z_down, y_up, y_down):
        signal(dev)
    pl.semaphore_wait(barrier, 7)

    def greet(n):
        for k, dev in enumerate((z_up, z_down) + ((y_up, y_down) if n == 0 else ())):
            pl.semaphore_signal(here.at[4 * n + k], inc=1, device_id=dev,
                                device_id_type=pl.DeviceIdType.MESH)

    def greeted(n):
        for k in range(4 if n == 0 else 2):
            pl.semaphore_wait(here.at[4 * n + k], 1)

    greet(0)
    sends = []

    def go(copy):
        copy.start()
        sends.append(copy)

    HALF = ROWS // 2

    def tok_copy(n, slot, half, dev):
        ref = tok.at[slot, pl.ds(half * HALF, HALF)]
        return remote(ref, ref, tok_send.at[n], tok_recv.at[2 * slot + half], dev)

    def tok_go(slot, half, dev):
        go(tok_copy(len(sends), slot, half, dev))

    def tok_wait(slot):
        for half in range(2):
            tok_copy(0, slot, half, partner).wait_recv()

    def slot(xx, cc, f):
        return (2 * xx + cc) * 2 + f

    loads[0].wait()
    for half in range(2):
        tok_go(slot(x, mine, 0), half, right)
    loads[1].wait()
    for half in range(2):
        tok_go(slot(x, mine, 1), half, left)
    for f in range(2):
        for half in range(2):
            tok_go(slot(x, mine, f), half, partner)
    for half in range(2):
        tok_go(slot(x, mine, 1), half, right)
        tok_go(slot(x, mine, 0), half, left)

    rates = [rate_ref[2 * tp + h] for h in range(2)]
    pos = lax.broadcasted_iota(jnp.int32, (ROWS, HD), 0).astype(F32)
    gap = (lax.broadcasted_iota(jnp.int32, (HD, ROWS), 0) + (ROWS - HD)
           - lax.broadcasted_iota(jnp.int32, (HD, ROWS), 1))
    lower = gap >= 0
    gap_f = jnp.where(lower, gap, 0).astype(F32)
    for h in range(2):
        tail[h] = jnp.exp(-rates[h] * (ROWS - 1.0 - pos))
        lead[h] = jnp.exp(-rates[h] * (pos + 1.0))
        mask[h] = jnp.where(lower, jnp.exp(-rates[h] * gap_f), 0.0)

    def project(s1, s2, first=False, lo=0, hi=4, squares=True):
        rows1 = pl.ds(pl.multiple_of(s1 * CH, CH), CH)
        rows2 = pl.ds(pl.multiple_of(s2 * CH, CH), CH)

        def body(j, carry):
            part = jnp.dot(tok[s1], w[j, rows1, :], preferred_element_type=F32)
            part += jnp.dot(tok[s2], w[j, rows2, :], preferred_element_type=F32)
            if first:
                acc[j] = part
            else:
                acc[j] += part
            return carry

        lax.fori_loop(lo, hi, body, 0)
        if not squares:
            return
        a = tok[s1].astype(F32)
        b = tok[s2].astype(F32)
        a = a * a
        b = b * b
        total = (a[:, :HD] + a[:, HD:]) + (b[:, :HD] + b[:, HD:])
        if first:
            sq[...] = total
        else:
            sq[...] += total

    def pass_on(s_left, s_right, forward):
        for half in range(2):
            tok_copy(0, s_left, half, partner).wait_recv()
            if forward:
                tok_go(s_left, half, right)
            tok_go(s_left, half, partner)
            tok_copy(0, s_right, half, partner).wait_recv()
            if forward:
                tok_go(s_right, half, left)
            tok_go(s_right, half, partner)

    for c in loads[2:6]:
        c.wait()
    project(slot(x, mine, 0), slot(x, mine, 1), True)
    greeted(0)
    greet(1)
    tok_wait(slot(x, other, 0))
    tok_wait(slot(x, other, 1))
    project(slot(x, other, 0), slot(x, other, 1))

    pass_on(slot(xl, mine, 0), slot(xr, mine, 1), True)
    project(slot(xl, mine, 0), slot(xr, mine, 1))
    greeted(1)
    greet(2)
    tok_wait(slot(xl, other, 0))
    tok_wait(slot(xr, other, 1))
    project(slot(xl, other, 0), slot(xr, other, 1))

    pass_on(slot(xl, mine, 1), slot(xr, mine, 0), False)
    project(slot(xl, mine, 1), slot(xr, mine, 0))
    tok_wait(slot(xl, other, 1))
    tok_wait(slot(xr, other, 0))
    project(slot(xl, other, 1), slot(xr, other, 0))

    pass_on(slot(xo, mine, 0), slot(xo, mine, 1), False)
    project(slot(xo, mine, 0), slot(xo, mine, 1))
    tok_wait(slot(xo, other, 0))
    tok_wait(slot(xo, other, 1))
    last = (slot(xo, other, 0), slot(xo, other, 1))
    project(*last, lo=1, hi=3)
    greeted(2)

    inv = lax.rsqrt(jnp.sum(sq[...], axis=1, keepdims=True) / float(WIDTH) + 1e-06)
    kb[...] = silu(acc[1] * inv).astype(BF)
    vb[...] = (acc[2] * inv).astype(BF)

    for h in range(2):
        cols = slice(h * HD, (h + 1) * HD)
        scaled = (kb[:, cols].astype(F32) * tail[h]).astype(BF)
        state = lax.dot_general(scaled, vb[:, cols], (((0,), (0,)), ((), ())),
                                preferred_element_type=F32)
        lsend[h * 4:(h + 1) * 4] = state.astype(BF).reshape(4, 32, HD)

    far_first = (4, 3, 5, 2, 6, 1, 7)
    for n, d in enumerate(far_first):
        zz = (z + d) % NZ
        go(remote(lsend.at[zz], r1.at[z], s1s.at[n], s1r.at[z], (y * NZ + zz, tp)))
    r1[z] = lsend[z]

    project(*last, lo=0, hi=1, squares=False)
    qb[...] = silu(acc[0] * inv).astype(BF)

    def attend(h):
        cols = slice(h * HD, (h + 1) * HD)
        for i in range(4):
            n = (i + 1) * HD
            rows = slice(i * HD, n)
            scores = lax.dot_general(qb[rows, cols], kb[0:n, cols], (((1,), (1,)), ((), ())),
                                     preferred_element_type=F32)
            weights = (scores * mask[h, :, ROWS - n:]).astype(BF)
            intra[rows, cols] = jnp.dot(weights, vb[0:n, cols], preferred_element_type=F32)

    attend(0)
    for d in far_first[::-1]:
        zz = (z + d) % NZ
        remote(lsend.at[zz], r1.at[zz], s1s.at[0], s1r.at[zz], partner).wait_recv()
    rate_z = rate_ref[2 * tp + z // 4]
    step = jnp.exp(jnp.full((1, HD), -rate_z * ROWS, F32))
    run = jnp.zeros((32, HD), F32)
    before = []
    for k in range(NZ):
        before.append(run)
        run = step * run + r1[k].astype(F32)
    rtsend[...] = run
    for n, d in enumerate((2, 1, 3)):
        yy = (y + d) % NY
        go(remote(rtsend, rt.at[y], s2s.at[n], s2r.at[y], (yy * NZ + z, tp)))
    rt[y] = run
    attend(1)
    for d in (1, 3, 2):
        yy = (y + d) % NY
        remote(rtsend, rt.at[yy], s2s.at[0], s2r.at[yy], partner).wait_recv()
    start = jnp.zeros((32, HD), F32)
    for k in range(NY):
        gone = jnp.maximum(y - 1 - k, 0).astype(F32) * float(NZ * ROWS)
        factor = jnp.exp(jnp.full((1, HD), -rate_z * gone, F32))
        start += jnp.where(k < y, factor, 0.0) * rt[k]
    for k in range(NZ):
        factor = jnp.exp(jnp.full((1, HD), -rate_z * float(k * ROWS), F32))
        ssend[k] = (before[k] + factor * start).astype(BF)
    for n, d in enumerate(far_first):
        zz = (z + d) % NZ
        go(remote(ssend.at[zz], srecv.at[z], s3s.at[n], s3r.at[z], (y * NZ + zz, tp)))
    srecv[z] = ssend[z]
    project(*last, lo=3, hi=4, squares=False)
    gate[...] = silu(acc[3] * inv)
    loads[6].wait()
    loads[7].wait()
    for d in far_first[::-1]:
        zz = (z + d) % NZ
        remote(ssend.at[zz], srecv.at[zz], s3s.at[0], s3r.at[zz], partner).wait_recv()
    parts = []
    offset = (ROWS * seq).astype(F32)
    for h in range(2):
        incoming = srecv[h * 4:(h + 1) * 4].astype(F32).reshape(HD, HD)
        incoming += jnp.exp(jnp.full((1, HD), -rates[h] * offset, F32)) * stv[h]
        high = incoming.astype(BF)
        parts.append((high, (incoming - high.astype(F32)).astype(BF)))

    QUARTER = ROWS // 4
    first_hid = len(sends)

    def hid_copy(n, sl, part, dev):
        ref = hid.at[sl, pl.ds(part * QUARTER, QUARTER)]
        return remote(ref, ref, hid_send.at[n], hid_recv.at[4 * sl + part], dev)

    def hid_go(sl, part, *devs):
        for dev in devs:
            go(hid_copy(len(sends) - first_hid, sl, part, dev))

    def hid_wait(sl, part):
        hid_copy(0, sl, part, partner).wait_recv()

    for part in (0, 2, 1, 3):
        rows = slice(part * QUARTER, (part + 1) * QUARTER)
        for h in range(2):
            cols = slice(h * HD, (h + 1) * HD)
            q = qb[rows, cols]
            inter = jnp.dot(q, parts[h][0], preferred_element_type=F32)
            inter += jnp.dot(q, parts[h][1], preferred_element_type=F32)
            att = intra[rows, cols] + lead[h, rows, :] * inter
            norm = lax.rsqrt(jnp.mean(att * att, axis=1, keepdims=True) + 1e-06)
            hid[tp, rows, cols] = (att * norm * gate[rows, cols]).astype(BF)
        hid_go(tp, part, right if part < 2 else left, partner)
    for i in range(2):
        hid_go(tp, 2 + i, right)
        hid_go(tp, i, left)

    def out_part(sl, half, first=False):
        rows = slice(half * HALF, (half + 1) * HALF)
        part = jnp.dot(hid[sl, rows, :], wov[pl.ds(pl.multiple_of(sl * CH, CH), CH), :],
                       preferred_element_type=F32)
        if first:
            oacc[rows, :] = part
        else:
            oacc[rows, :] += part

    def arrived(sl, half):
        hid_wait(sl, 2 * half)
        hid_wait(sl, 2 * half + 1)
        out_part(sl, half)

    tl, tr, to = 2 * xl, 2 * xr, 2 * xo
    tpp = 2 * x + other
    out_part(tp, 0, True)
    out_part(tp, 1, True)
    arrived(tpp, 0)
    arrived(tpp, 1)

    for i in range(2):
        hid_wait(tl + mine, i)
        hid_go(tl + mine, i, right, partner)
        hid_wait(tr + mine, 2 + i)
        hid_go(tr + mine, 2 + i, left, partner)
    out_part(tl + mine, 0)
    out_part(tr + mine, 1)
    arrived(tl + other, 0)
    arrived(tr + other, 1)

    for i in range(2):
        hid_wait(tl + mine, 2 + i)
        hid_go(tl + mine, 2 + i, partner)
        hid_wait(tr + mine, i)
        hid_go(tr + mine, i, partner)
    out_part(tl + mine, 1)
    out_part(tr + mine, 0)
    arrived(tl + other, 1)
    arrived(tr + other, 0)

    for i in range(2):
        hid_wait(to + mine, i)
        hid_go(to + mine, i, partner)
        hid_wait(to + mine, 2 + i)
        hid_go(to + mine, 2 + i, partner)
    out_part(to + mine, 0)
    out_part(to + mine, 1)
    arrived(to + other, 0)
    arrived(to + other, 1)

    for f in range(2):
        cols = slice(f * CH, (f + 1) * CH)
        out_ref[:, cols] = (tok[2 * tp + f].astype(F32) + oacc[:, cols]).astype(BF)
    for c in sends:
        c.wait_send()


def per_device(tokens, w_query, w_key, w_value, w_gate, w_out, decay_rate, state_in):
    anyspec = pl.BlockSpec(memory_space=pl.ANY)
    dma = pltpu.SemaphoreType.DMA
    return pl.pallas_call(
        kernel,
        out_shape=jax.ShapeDtypeStruct((ROWS, 512), BF),
        in_specs=[anyspec] * 6 + [pl.BlockSpec(memory_space=pltpu.SMEM), anyspec],
        out_specs=pl.BlockSpec(memory_space=pltpu.VMEM),
        scratch_shapes=[
            pltpu.VMEM((16, ROWS, CH), BF),
            pltpu.VMEM((4, WIDTH, 256), BF),
            pltpu.VMEM((2048, 512), BF),
            pltpu.VMEM((2, HD, HD), F32),
            pltpu.VMEM((4, ROWS, 256), F32),
            pltpu.VMEM((ROWS, HD), F32),
            pltpu.VMEM((2, HD, ROWS), F32),
            pltpu.VMEM((2, ROWS, HD), F32),
            pltpu.VMEM((2, ROWS, HD), F32),
            pltpu.VMEM((ROWS, 256), BF),
            pltpu.VMEM((ROWS, 256), BF),
            pltpu.VMEM((ROWS, 256), BF),
            pltpu.VMEM((ROWS, 256), F32),
            pltpu.VMEM((ROWS, 256), F32),
            pltpu.VMEM((NZ, 32, HD), BF),
            pltpu.VMEM((NZ, 32, HD), BF),
            pltpu.VMEM((32, HD), F32),
            pltpu.VMEM((NY, 32, HD), F32),
            pltpu.VMEM((NZ, 32, HD), BF),
            pltpu.VMEM((NZ, 32, HD), BF),
            pltpu.VMEM((8, ROWS, 256), BF),
            pltpu.VMEM((ROWS, 512), F32),
            dma((8,)), dma((28,)), dma((32,)), dma((7,)), dma((8,)), dma((3,)), dma((4,)),
            dma((7,)), dma((8,)), dma((28,)), dma((32,)),
            pltpu.SemaphoreType.REGULAR((10,)),
        ],
        compiler_params=pltpu.CompilerParams(
            collective_id=0, has_side_effects=True, vmem_limit_bytes=56 * 1024 * 1024),
        name="lightning_layer",
    )(tokens, w_query, w_key, w_value, w_gate, w_out, decay_rate, state_in)


def solution(mesh):
    return jax.shard_map(
        per_device,
        mesh=mesh,
        in_specs=(
            P("seq", "tp"),
            P(None, "tp"),
            P(None, "tp"),
            P(None, "tp"),
            P(None, "tp"),
            P(None, "tp"),
            P(),
            P("tp", None, None),
        ),
        out_specs=P("seq", "tp"),
        check_vma=False,
    )
```

```python
import jax
import jax.numpy as jnp
from jax import lax
from jax.experimental import pallas as pl
from jax.experimental.pallas import tpu as pltpu
from jax.sharding import PartitionSpec as P

NX, NY, NZ = 4, 4, 8
ROWS = 512
WIDTH = 4096
HD = 128
CH = 256
BF = jnp.bfloat16
F32 = jnp.float32


def silu(z):
    return z / (1.0 + jnp.exp(-z))


def kernel(tok_in, wq, wk, wv, wg, wo, rate_ref, st_in, out_ref,
           tok, w, wov, stv, acc, sq, mask, tail, lead, kb, vb, qb, gate, intra,
           lsend, r1, rtsend, rt, ssend, srecv, hid, oacc,
           load_sem, tok_send, tok_recv, s1s, s1r, s2s, s2r, s3s, s3r, hid_send, hid_recv, here):
    tp = lax.axis_index("tp")
    seq = lax.axis_index("seq")
    x, core = tp // 2, tp % 2
    y, z = seq // NZ, seq % NZ
    xr, xl, xo = (x + 1) % NX, (x + 3) % NX, (x + 2) % NX
    right, left = (seq, 2 * xr + core), (seq, 2 * xl + core)
    partner = (seq, 2 * x + 1 - core)
    mine, other = core, 1 - core

    def signal(dev):
        pl.semaphore_signal(barrier, inc=1, device_id=dev, device_id_type=pl.DeviceIdType.MESH)

    def remote(src, dst, ss, rs, dev):
        return pltpu.make_async_remote_copy(
            src_ref=src, dst_ref=dst, send_sem=ss, recv_sem=rs, device_id=dev,
            device_id_type=pl.DeviceIdType.MESH)

    loads = []
    for f in range(2):
        loads.append(pltpu.make_async_copy(
            tok_in.at[:, pl.ds(f * CH, CH)], tok.at[2 * tp + f], load_sem.at[f]))
    for j, ref in enumerate((wq, wk, wv, wg)):
        loads.append(pltpu.make_async_copy(ref, w.at[j], load_sem.at[2 + j]))
    loads.append(pltpu.make_async_copy(wo, wov, load_sem.at[6]))
    loads.append(pltpu.make_async_copy(st_in, stv, load_sem.at[7]))
    for c in loads:
        c.start()

    barrier = pltpu.get_barrier_semaphore()
    z_up, z_down = (y * NZ + (z + 1) % NZ, tp), (y * NZ + (z + NZ - 1) % NZ, tp)
    y_up, y_down = (((y + 1) % NY) * NZ + z, tp), (((y + NY - 1) % NY) * NZ + z, tp)
    for dev in (right, left, partner, z_up, z_down, y_up, y_down):
        signal(dev)
    pl.semaphore_wait(barrier, 7)

    def greet(n):
        for k, dev in enumerate((z_up, z_down) + ((y_up, y_down) if n == 0 else ())):
            pl.semaphore_signal(here.at[4 * n + k], inc=1, device_id=dev,
                                device_id_type=pl.DeviceIdType.MESH)

    def greeted(n):
        for k in range(4 if n == 0 else 2):
            pl.semaphore_wait(here.at[4 * n + k], 1)

    greet(0)
    sends = []

    def go(copy):
        copy.start()
        sends.append(copy)

    HALF = ROWS // 2

    def tok_copy(n, slot, half, dev):
        ref = tok.at[slot, pl.ds(half * HALF, HALF)]
        return remote(ref, ref, tok_send.at[n], tok_recv.at[2 * slot + half], dev)

    def tok_go(slot, half, dev):
        go(tok_copy(len(sends), slot, half, dev))

    def tok_wait(slot):
        for half in range(2):
            tok_copy(0, slot, half, partner).wait_recv()

    def slot(xx, cc, f):
        return (2 * xx + cc) * 2 + f

    loads[0].wait()
    for half in range(2):
        tok_go(slot(x, mine, 0), half, right)
    loads[1].wait()
    for half in range(2):
        tok_go(slot(x, mine, 1), half, left)
    for f in range(2):
        for half in range(2):
            tok_go(slot(x, mine, f), half, partner)
    for half in range(2):
        tok_go(slot(x, mine, 1), half, right)
        tok_go(slot(x, mine, 0), half, left)

    rates = [rate_ref[2 * tp + h] for h in range(2)]
    pos = lax.broadcasted_iota(jnp.int32, (ROWS, HD), 0).astype(F32)
    gap = (lax.broadcasted_iota(jnp.int32, (HD, ROWS), 0) + (ROWS - HD)
           - lax.broadcasted_iota(jnp.int32, (HD, ROWS), 1))
    lower = gap >= 0
    gap_f = jnp.where(lower, gap, 0).astype(F32)
    for h in range(2):
        tail[h] = jnp.exp(-rates[h] * (ROWS - 1.0 - pos))
        lead[h] = jnp.exp(-rates[h] * (pos + 1.0))
        mask[h] = jnp.where(lower, jnp.exp(-rates[h] * gap_f), 0.0)

    def project(s1, s2, first=False, lo=0, hi=4, squares=True):
        rows1 = pl.ds(pl.multiple_of(s1 * CH, CH), CH)
        rows2 = pl.ds(pl.multiple_of(s2 * CH, CH), CH)

        def body(j, carry):
            part = jnp.dot(tok[s1], w[j, rows1, :], preferred_element_type=F32)
            part += jnp.dot(tok[s2], w[j, rows2, :], preferred_element_type=F32)
            if first:
                acc[j] = part
            else:
                acc[j] += part
            return carry

        lax.fori_loop(lo, hi, body, 0)
        if not squares:
            return
        a = tok[s1].astype(F32)
        b = tok[s2].astype(F32)
        a = a * a
        b = b * b
        total = (a[:, :HD] + a[:, HD:]) + (b[:, :HD] + b[:, HD:])
        if first:
            sq[...] = total
        else:
            sq[...] += total

    def pass_on(s_left, s_right, forward):
        for half in range(2):
            tok_copy(0, s_left, half, partner).wait_recv()
            if forward:
                tok_go(s_left, half, right)
            tok_go(s_left, half, partner)
            tok_copy(0, s_right, half, partner).wait_recv()
            if forward:
                tok_go(s_right, half, left)
            tok_go(s_right, half, partner)

    for c in loads[2:6]:
        c.wait()
    project(slot(x, mine, 0), slot(x, mine, 1), True)
    greeted(0)
    greet(1)
    tok_wait(slot(x, other, 0))
    tok_wait(slot(x, other, 1))
    project(slot(x, other, 0), slot(x, other, 1))

    pass_on(slot(xl, mine, 0), slot(xr, mine, 1), True)
    project(slot(xl, mine, 0), slot(xr, mine, 1))
    greeted(1)
    greet(2)
    tok_wait(slot(xl, other, 0))
    tok_wait(slot(xr, other, 1))
    project(slot(xl, other, 0), slot(xr, other, 1))

    pass_on(slot(xl, mine, 1), slot(xr, mine, 0), False)
    project(slot(xl, mine, 1), slot(xr, mine, 0))
    tok_wait(slot(xl, other, 1))
    tok_wait(slot(xr, other, 0))
    project(slot(xl, other, 1), slot(xr, other, 0))

    pass_on(slot(xo, mine, 0), slot(xo, mine, 1), False)
    project(slot(xo, mine, 0), slot(xo, mine, 1))
    tok_wait(slot(xo, other, 0))
    tok_wait(slot(xo, other, 1))
    last = (slot(xo, other, 0), slot(xo, other, 1))
    project(*last, lo=1, hi=3)
    greeted(2)

    inv = lax.rsqrt(jnp.sum(sq[...], axis=1, keepdims=True) / float(WIDTH) + 1e-06)
    kb[...] = silu(acc[1] * inv).astype(BF)
    vb[...] = (acc[2] * inv).astype(BF)

    for h in range(2):
        cols = slice(h * HD, (h + 1) * HD)
        scaled = (kb[:, cols].astype(F32) * tail[h]).astype(BF)
        state = lax.dot_general(scaled, vb[:, cols], (((0,), (0,)), ((), ())),
                                preferred_element_type=F32)
        lsend[h * 4:(h + 1) * 4] = state.astype(BF).reshape(4, 32, HD)

    far_first = (4, 3, 5, 2, 6, 1, 7)
    for n, d in enumerate(far_first):
        zz = (z + d) % NZ
        go(remote(lsend.at[zz], r1.at[z], s1s.at[n], s1r.at[z], (y * NZ + zz, tp)))
    r1[z] = lsend[z]

    project(*last, lo=0, hi=1, squares=False)
    qb[...] = silu(acc[0] * inv).astype(BF)

    def attend(h):
        cols = slice(h * HD, (h + 1) * HD)
        for i in range(4):
            n = (i + 1) * HD
            rows = slice(i * HD, n)
            scores = lax.dot_general(qb[rows, cols], kb[0:n, cols], (((1,), (1,)), ((), ())),
                                     preferred_element_type=F32)
            weights = (scores * mask[h, :, ROWS - n:]).astype(BF)
            intra[rows, cols] = jnp.dot(weights, vb[0:n, cols], preferred_element_type=F32)

    attend(0)
    for d in far_first[::-1]:
        zz = (z + d) % NZ
        remote(lsend.at[zz], r1.at[zz], s1s.at[0], s1r.at[zz], partner).wait_recv()
    rate_z = rate_ref[2 * tp + z // 4]
    step = jnp.exp(jnp.full((1, HD), -rate_z * ROWS, F32))
    run = jnp.zeros((32, HD), F32)
    before = []
    for k in range(NZ):
        before.append(run)
        run = step * run + r1[k].astype(F32)
    rtsend[...] = run
    for n, d in enumerate((2, 1, 3)):
        yy = (y + d) % NY
        go(remote(rtsend, rt.at[y], s2s.at[n], s2r.at[y], (yy * NZ + z, tp)))
    rt[y] = run
    attend(1)
    for d in (1, 3, 2):
        yy = (y + d) % NY
        remote(rtsend, rt.at[yy], s2s.at[0], s2r.at[yy], partner).wait_recv()
    start = jnp.zeros((32, HD), F32)
    for k in range(NY):
        gone = jnp.maximum(y - 1 - k, 0).astype(F32) * float(NZ * ROWS)
        factor = jnp.exp(jnp.full((1, HD), -rate_z * gone, F32))
        start += jnp.where(k < y, factor, 0.0) * rt[k]
    for k in range(NZ):
        factor = jnp.exp(jnp.full((1, HD), -rate_z * float(k * ROWS), F32))
        ssend[k] = (before[k] + factor * start).astype(BF)
    for n, d in enumerate(far_first):
        zz = (z + d) % NZ
        go(remote(ssend.at[zz], srecv.at[z], s3s.at[n], s3r.at[z], (y * NZ + zz, tp)))
    srecv[z] = ssend[z]
    project(*last, lo=3, hi=4, squares=False)
    gate[...] = silu(acc[3] * inv)
    loads[6].wait()
    loads[7].wait()
    for d in far_first[::-1]:
        zz = (z + d) % NZ
        remote(ssend.at[zz], srecv.at[zz], s3s.at[0], s3r.at[zz], partner).wait_recv()
    parts = []
    offset = (ROWS * seq).astype(F32)
    for h in range(2):
        incoming = srecv[h * 4:(h + 1) * 4].astype(F32).reshape(HD, HD)
        incoming += jnp.exp(jnp.full((1, HD), -rates[h] * offset, F32)) * stv[h]
        high = incoming.astype(BF)
        parts.append((high, (incoming - high.astype(F32)).astype(BF)))

    QUARTER = ROWS // 4
    first_hid = len(sends)

    def hid_copy(n, sl, part, dev):
        ref = hid.at[sl, pl.ds(part * QUARTER, QUARTER)]
        return remote(ref, ref, hid_send.at[n], hid_recv.at[4 * sl + part], dev)

    def hid_go(sl, part, *devs):
        for dev in devs:
            go(hid_copy(len(sends) - first_hid, sl, part, dev))

    def hid_wait(sl, part):
        hid_copy(0, sl, part, partner).wait_recv()

    for part in (0, 2, 1, 3):
        rows = slice(part * QUARTER, (part + 1) * QUARTER)
        for h in range(2):
            cols = slice(h * HD, (h + 1) * HD)
            q = qb[rows, cols]
            inter = jnp.dot(q, parts[h][0], preferred_element_type=F32)
            inter += jnp.dot(q, parts[h][1], preferred_element_type=F32)
            att = intra[rows, cols] + lead[h, rows, :] * inter
            norm = lax.rsqrt(jnp.mean(att * att, axis=1, keepdims=True) + 1e-06)
            hid[tp, rows, cols] = (att * norm * gate[rows, cols]).astype(BF)
        hid_go(tp, part, right if part < 2 else left, partner)
    for i in range(2):
        hid_go(tp, 2 + i, right)
        hid_go(tp, i, left)

    def out_part(sl, half, first=False):
        rows = slice(half * HALF, (half + 1) * HALF)
        part = jnp.dot(hid[sl, rows, :], wov[pl.ds(pl.multiple_of(sl * CH, CH), CH), :],
                       preferred_element_type=F32)
        if first:
            oacc[rows, :] = part
        else:
            oacc[rows, :] += part

    def arrived(sl, half):
        hid_wait(sl, 2 * half)
        hid_wait(sl, 2 * half + 1)
        out_part(sl, half)

    tl, tr, to = 2 * xl, 2 * xr, 2 * xo
    tpp = 2 * x + other
    out_part(tp, 0, True)
    out_part(tp, 1, True)
    arrived(tpp, 0)
    arrived(tpp, 1)

    for i in range(2):
        hid_wait(tl + mine, i)
        hid_go(tl + mine, i, right, partner)
        hid_wait(tr + mine, 2 + i)
        hid_go(tr + mine, 2 + i, left, partner)
    out_part(tl + mine, 0)
    out_part(tr + mine, 1)
    arrived(tl + other, 0)
    arrived(tr + other, 1)

    for i in range(2):
        hid_wait(tl + mine, 2 + i)
        hid_go(tl + mine, 2 + i, partner)
        hid_wait(tr + mine, i)
        hid_go(tr + mine, i, partner)
    out_part(tl + mine, 1)
    out_part(tr + mine, 0)
    arrived(tl + other, 1)
    arrived(tr + other, 0)

    for i in range(2):
        hid_wait(to + mine, i)
        hid_go(to + mine, i, partner)
        hid_wait(to + mine, 2 + i)
        hid_go(to + mine, 2 + i, partner)
    out_part(to + mine, 0)
    out_part(to + mine, 1)
    arrived(to + other, 0)
    arrived(to + other, 1)

    for f in range(2):
        cols = slice(f * CH, (f + 1) * CH)
        out_ref[:, cols] = (tok[2 * tp + f].astype(F32) + oacc[:, cols]).astype(BF)
    for c in sends:
        c.wait_send()


def per_device(tokens, w_query, w_key, w_value, w_gate, w_out, decay_rate, state_in):
    anyspec = pl.BlockSpec(memory_space=pl.ANY)
    dma = pltpu.SemaphoreType.DMA
    return pl.pallas_call(
        kernel,
        out_shape=pltpu.VMEM((ROWS, 512), BF),
        in_specs=[anyspec] * 6 + [pl.BlockSpec(memory_space=pltpu.SMEM), anyspec],
        out_specs=pl.BlockSpec(memory_space=pltpu.VMEM),
        scratch_shapes=[
            pltpu.VMEM((16, ROWS, CH), BF),
            pltpu.VMEM((4, WIDTH, 256), BF),
            pltpu.VMEM((2048, 512), BF),
            pltpu.VMEM((2, HD, HD), F32),
            pltpu.VMEM((4, ROWS, 256), F32),
            pltpu.VMEM((ROWS, HD), F32),
            pltpu.VMEM((2, HD, ROWS), F32),
            pltpu.VMEM((2, ROWS, HD), F32),
            pltpu.VMEM((2, ROWS, HD), F32),
            pltpu.VMEM((ROWS, 256), BF),
            pltpu.VMEM((ROWS, 256), BF),
            pltpu.VMEM((ROWS, 256), BF),
            pltpu.VMEM((ROWS, 256), F32),
            pltpu.VMEM((ROWS, 256), F32),
            pltpu.VMEM((NZ, 32, HD), BF),
            pltpu.VMEM((NZ, 32, HD), BF),
            pltpu.VMEM((32, HD), F32),
            pltpu.VMEM((NY, 32, HD), F32),
            pltpu.VMEM((NZ, 32, HD), BF),
            pltpu.VMEM((NZ, 32, HD), BF),
            pltpu.VMEM((8, ROWS, 256), BF),
            pltpu.VMEM((ROWS, 512), F32),
            dma((8,)), dma((28,)), dma((32,)), dma((7,)), dma((8,)), dma((3,)), dma((4,)),
            dma((7,)), dma((8,)), dma((28,)), dma((32,)),
            pltpu.SemaphoreType.REGULAR((10,)),
        ],
        compiler_params=pltpu.CompilerParams(
            collective_id=0, has_side_effects=True, vmem_limit_bytes=56 * 1024 * 1024),
        name="lightning_layer",
    )(tokens, w_query, w_key, w_value, w_gate, w_out, decay_rate, state_in)


def solution(mesh):
    return jax.shard_map(
        per_device,
        mesh=mesh,
        in_specs=(
            P("seq", "tp"),
            P(None, "tp"),
            P(None, "tp"),
            P(None, "tp"),
            P(None, "tp"),
            P(None, "tp"),
            P(),
            P("tp", None, None),
        ),
        out_specs=P("seq", "tp"),
        check_vma=False,
    )
```

```python
import jax
import jax.numpy as jnp
from jax import lax
from jax.experimental import pallas as pl
from jax.experimental.pallas import tpu as pltpu
from jax.sharding import PartitionSpec as P

NX, NY, NZ = 4, 4, 8
ROWS = 512
WIDTH = 4096
HD = 128
CH = 256
BF = jnp.bfloat16
F32 = jnp.float32


def silu(z):
    return z / (1.0 + jnp.exp(-z))


def kernel(tok_in, wq, wk, wv, wg, wo, rate_ref, st_in, out_ref,
           tok, w, wov, stv, acc, sq, mask, tail, lead, kb, vb, qb, gate, intra,
           lsend, r1, rtsend, rt, ssend, srecv, hid, oacc,
           load_sem, tok_send, tok_recv, s1s, s1r, s2s, s2r, s3s, s3r, hid_send, hid_recv, here):
    tp = lax.axis_index("tp")
    seq = lax.axis_index("seq")
    x, core = tp // 2, tp % 2
    y, z = seq // NZ, seq % NZ
    xr, xl, xo = (x + 1) % NX, (x + 3) % NX, (x + 2) % NX
    right, left = (seq, 2 * xr + core), (seq, 2 * xl + core)
    partner = (seq, 2 * x + 1 - core)
    mine, other = core, 1 - core

    def signal(dev):
        pl.semaphore_signal(barrier, inc=1, device_id=dev, device_id_type=pl.DeviceIdType.MESH)

    def remote(src, dst, ss, rs, dev):
        return pltpu.make_async_remote_copy(
            src_ref=src, dst_ref=dst, send_sem=ss, recv_sem=rs, device_id=dev,
            device_id_type=pl.DeviceIdType.MESH)

    loads = []
    for f in range(2):
        loads.append(pltpu.make_async_copy(
            tok_in.at[:, pl.ds(f * CH, CH)], tok.at[2 * tp + f], load_sem.at[f]))
    for j, ref in enumerate((wq, wk, wv, wg)):
        loads.append(pltpu.make_async_copy(ref, w.at[j], load_sem.at[2 + j]))
    loads.append(pltpu.make_async_copy(wo, wov, load_sem.at[6]))
    loads.append(pltpu.make_async_copy(st_in, stv, load_sem.at[7]))
    for c in loads:
        c.start()

    barrier = pltpu.get_barrier_semaphore()
    z_up, z_down = (y * NZ + (z + 1) % NZ, tp), (y * NZ + (z + NZ - 1) % NZ, tp)
    y_up, y_down = (((y + 1) % NY) * NZ + z, tp), (((y + NY - 1) % NY) * NZ + z, tp)
    for dev in (right, left, partner, z_up, z_down, y_up, y_down):
        signal(dev)
    pl.semaphore_wait(barrier, 7)

    def greet(n):
        for k, dev in enumerate((z_up, z_down) + ((y_up, y_down) if n == 0 else ())):
            pl.semaphore_signal(here.at[4 * n + k], inc=1, device_id=dev,
                                device_id_type=pl.DeviceIdType.MESH)

    def greeted(n):
        for k in range(4 if n == 0 else 2):
            pl.semaphore_wait(here.at[4 * n + k], 1)

    greet(0)
    sends = []

    def go(copy):
        copy.start()
        sends.append(copy)

    HALF = ROWS // 2

    def tok_copy(n, slot, half, dev):
        ref = tok.at[slot, pl.ds(half * HALF, HALF)]
        return remote(ref, ref, tok_send.at[n], tok_recv.at[2 * slot + half], dev)

    def tok_go(slot, half, dev):
        go(tok_copy(len(sends), slot, half, dev))

    def tok_wait(slot):
        for half in range(2):
            tok_copy(0, slot, half, partner).wait_recv()

    def slot(xx, cc, f):
        return (2 * xx + cc) * 2 + f

    loads[0].wait()
    for half in range(2):
        tok_go(slot(x, mine, 0), half, right)
    loads[1].wait()
    for half in range(2):
        tok_go(slot(x, mine, 1), half, left)
    for f in range(2):
        for half in range(2):
            tok_go(slot(x, mine, f), half, partner)
    for half in range(2):
        tok_go(slot(x, mine, 1), half, right)
        tok_go(slot(x, mine, 0), half, left)

    rates = [rate_ref[2 * tp + h] for h in range(2)]
    pos = lax.broadcasted_iota(jnp.int32, (ROWS, HD), 0).astype(F32)
    gap = (lax.broadcasted_iota(jnp.int32, (HD, ROWS), 0) + (ROWS - HD)
           - lax.broadcasted_iota(jnp.int32, (HD, ROWS), 1))
    lower = gap >= 0
    gap_f = jnp.where(lower, gap, 0).astype(F32)
    for h in range(2):
        tail[h] = jnp.exp(-rates[h] * (ROWS - 1.0 - pos))
        lead[h] = jnp.exp(-rates[h] * (pos + 1.0))
        mask[h] = jnp.where(lower, jnp.exp(-rates[h] * gap_f), 0.0)

    def project(s1, s2, first=False, lo=0, hi=4, squares=True, r=slice(0, ROWS)):
        rows1 = pl.ds(pl.multiple_of(s1 * CH, CH), CH)
        rows2 = pl.ds(pl.multiple_of(s2 * CH, CH), CH)

        def body(j, carry):
            part = jnp.dot(tok[s1, r, :], w[j, rows1, :], preferred_element_type=F32)
            part += jnp.dot(tok[s2, r, :], w[j, rows2, :], preferred_element_type=F32)
            if first:
                acc[j, r, :] = part
            else:
                acc[j, r, :] += part
            return carry

        lax.fori_loop(lo, hi, body, 0)
        if not squares:
            return
        a = tok[s1, r, :].astype(F32)
        b = tok[s2, r, :].astype(F32)
        a = a * a
        b = b * b
        total = (a[:, :HD] + a[:, HD:]) + (b[:, :HD] + b[:, HD:])
        if first:
            sq[r, :] = total
        else:
            sq[r, :] += total

    def pass_on(s_left, s_right, forward):
        for half in range(2):
            tok_copy(0, s_left, half, partner).wait_recv()
            if forward:
                tok_go(s_left, half, right)
            tok_go(s_left, half, partner)
            tok_copy(0, s_right, half, partner).wait_recv()
            if forward:
                tok_go(s_right, half, left)
            tok_go(s_right, half, partner)

    for c in loads[2:6]:
        c.wait()
    project(slot(x, mine, 0), slot(x, mine, 1), True)
    greeted(0)
    greet(1)
    tok_wait(slot(x, other, 0))
    tok_wait(slot(x, other, 1))
    project(slot(x, other, 0), slot(x, other, 1))

    pass_on(slot(xl, mine, 0), slot(xr, mine, 1), True)
    project(slot(xl, mine, 0), slot(xr, mine, 1))
    greeted(1)
    greet(2)
    tok_wait(slot(xl, other, 0))
    tok_wait(slot(xr, other, 1))
    project(slot(xl, other, 0), slot(xr, other, 1))

    pass_on(slot(xl, mine, 1), slot(xr, mine, 0), False)
    project(slot(xl, mine, 1), slot(xr, mine, 0))
    tok_wait(slot(xl, other, 1))
    tok_wait(slot(xr, other, 0))
    project(slot(xl, other, 1), slot(xr, other, 0))

    last = [(slot(xo, c, 0), slot(xo, c, 1)) for c in (mine, other)]
    for half in range(2):
        r = slice(half * HALF, (half + 1) * HALF)
        for sl in last[0]:
            tok_copy(0, sl, half, partner).wait_recv()
            tok_go(sl, half, partner)
        project(*last[0], lo=1, hi=3, r=r)
        for sl in last[1]:
            tok_copy(0, sl, half, partner).wait_recv()
        project(*last[1], lo=1, hi=3, r=r)
    greeted(2)

    inv = lax.rsqrt(jnp.sum(sq[...], axis=1, keepdims=True) / float(WIDTH) + 1e-06)
    kb[...] = silu(acc[1] * inv).astype(BF)
    vb[...] = (acc[2] * inv).astype(BF)

    for h in range(2):
        cols = slice(h * HD, (h + 1) * HD)
        scaled = (kb[:, cols].astype(F32) * tail[h]).astype(BF)
        state = lax.dot_general(scaled, vb[:, cols], (((0,), (0,)), ((), ())),
                                preferred_element_type=F32)
        lsend[h * 4:(h + 1) * 4] = state.astype(BF).reshape(4, 32, HD)

    far_first = (4, 3, 5, 2, 6, 1, 7)
    for n, d in enumerate(far_first):
        zz = (z + d) % NZ
        go(remote(lsend.at[zz], r1.at[z], s1s.at[n], s1r.at[z], (y * NZ + zz, tp)))
    r1[z] = lsend[z]

    for pair in last:
        project(*pair, lo=0, hi=1, squares=False)
    qb[...] = silu(acc[0] * inv).astype(BF)

    def attend(h):
        cols = slice(h * HD, (h + 1) * HD)
        for i in range(4):
            n = (i + 1) * HD
            rows = slice(i * HD, n)
            scores = lax.dot_general(qb[rows, cols], kb[0:n, cols], (((1,), (1,)), ((), ())),
                                     preferred_element_type=F32)
            weights = (scores * mask[h, :, ROWS - n:]).astype(BF)
            intra[rows, cols] = jnp.dot(weights, vb[0:n, cols], preferred_element_type=F32)

    attend(0)
    for d in far_first[::-1]:
        zz = (z + d) % NZ
        remote(lsend.at[zz], r1.at[zz], s1s.at[0], s1r.at[zz], partner).wait_recv()
    rate_z = rate_ref[2 * tp + z // 4]
    step = jnp.exp(jnp.full((1, HD), -rate_z * ROWS, F32))
    run = jnp.zeros((32, HD), F32)
    before = []
    for k in range(NZ):
        before.append(run)
        run = step * run + r1[k].astype(F32)
    rtsend[...] = run
    for n, d in enumerate((2, 1, 3)):
        yy = (y + d) % NY
        go(remote(rtsend, rt.at[y], s2s.at[n], s2r.at[y], (yy * NZ + z, tp)))
    rt[y] = run
    attend(1)
    for d in (1, 3, 2):
        yy = (y + d) % NY
        remote(rtsend, rt.at[yy], s2s.at[0], s2r.at[yy], partner).wait_recv()
    start = jnp.zeros((32, HD), F32)
    for k in range(NY):
        gone = jnp.maximum(y - 1 - k, 0).astype(F32) * float(NZ * ROWS)
        factor = jnp.exp(jnp.full((1, HD), -rate_z * gone, F32))
        start += jnp.where(k < y, factor, 0.0) * rt[k]
    for k in range(NZ):
        factor = jnp.exp(jnp.full((1, HD), -rate_z * float(k * ROWS), F32))
        ssend[k] = (before[k] + factor * start).astype(BF)
    for n, d in enumerate(far_first):
        zz = (z + d) % NZ
        go(remote(ssend.at[zz], srecv.at[z], s3s.at[n], s3r.at[z], (y * NZ + zz, tp)))
    srecv[z] = ssend[z]
    for pair in last:
        project(*pair, lo=3, hi=4, squares=False)
    gate[...] = silu(acc[3] * inv)
    loads[6].wait()
    loads[7].wait()
    for d in far_first[::-1]:
        zz = (z + d) % NZ
        remote(ssend.at[zz], srecv.at[zz], s3s.at[0], s3r.at[zz], partner).wait_recv()
    parts = []
    offset = (ROWS * seq).astype(F32)
    for h in range(2):
        incoming = srecv[h * 4:(h + 1) * 4].astype(F32).reshape(HD, HD)
        incoming += jnp.exp(jnp.full((1, HD), -rates[h] * offset, F32)) * stv[h]
        high = incoming.astype(BF)
        parts.append((high, (incoming - high.astype(F32)).astype(BF)))

    QUARTER = ROWS // 4
    first_hid = len(sends)

    def hid_copy(n, sl, part, dev):
        ref = hid.at[sl, pl.ds(part * QUARTER, QUARTER)]
        return remote(ref, ref, hid_send.at[n], hid_recv.at[4 * sl + part], dev)

    def hid_go(sl, part, *devs):
        for dev in devs:
            go(hid_copy(len(sends) - first_hid, sl, part, dev))

    def hid_wait(sl, part):
        hid_copy(0, sl, part, partner).wait_recv()

    for part in (0, 2, 1, 3):
        rows = slice(part * QUARTER, (part + 1) * QUARTER)
        for h in range(2):
            cols = slice(h * HD, (h + 1) * HD)
            q = qb[rows, cols]
            inter = jnp.dot(q, parts[h][0], preferred_element_type=F32)
            inter += jnp.dot(q, parts[h][1], preferred_element_type=F32)
            att = intra[rows, cols] + lead[h, rows, :] * inter
            norm = lax.rsqrt(jnp.mean(att * att, axis=1, keepdims=True) + 1e-06)
            hid[tp, rows, cols] = (att * norm * gate[rows, cols]).astype(BF)
        hid_go(tp, part, right if part < 2 else left, partner)
    for i in range(2):
        hid_go(tp, 2 + i, right)
        hid_go(tp, i, left)

    def out_part(sl, half, first=False):
        rows = slice(half * HALF, (half + 1) * HALF)
        part = jnp.dot(hid[sl, rows, :], wov[pl.ds(pl.multiple_of(sl * CH, CH), CH), :],
                       preferred_element_type=F32)
        if first:
            oacc[rows, :] = part
        else:
            oacc[rows, :] += part

    def arrived(sl, half):
        hid_wait(sl, 2 * half)
        hid_wait(sl, 2 * half + 1)
        out_part(sl, half)

    tl, tr, to = 2 * xl, 2 * xr, 2 * xo
    tpp = 2 * x + other
    out_part(tp, 0, True)
    out_part(tp, 1, True)
    arrived(tpp, 0)
    arrived(tpp, 1)

    for i in range(2):
        hid_wait(tl + mine, i)
        hid_go(tl + mine, i, right, partner)
        hid_wait(tr + mine, 2 + i)
        hid_go(tr + mine, 2 + i, left, partner)
    out_part(tl + mine, 0)
    out_part(tr + mine, 1)
    arrived(tl + other, 0)
    arrived(tr + other, 1)

    for i in range(2):
        hid_wait(tl + mine, 2 + i)
        hid_go(tl + mine, 2 + i, partner)
        hid_wait(tr + mine, i)
        hid_go(tr + mine, i, partner)
    out_part(tl + mine, 1)
    out_part(tr + mine, 0)
    arrived(tl + other, 1)
    arrived(tr + other, 0)

    for i in range(2):
        hid_wait(to + mine, i)
        hid_go(to + mine, i, partner)
        hid_wait(to + mine, 2 + i)
        hid_go(to + mine, 2 + i, partner)
    out_part(to + mine, 0)
    out_part(to + mine, 1)
    arrived(to + other, 0)
    arrived(to + other, 1)

    for f in range(2):
        cols = slice(f * CH, (f + 1) * CH)
        out_ref[:, cols] = (tok[2 * tp + f].astype(F32) + oacc[:, cols]).astype(BF)
    for c in sends:
        c.wait_send()


def per_device(tokens, w_query, w_key, w_value, w_gate, w_out, decay_rate, state_in):
    anyspec = pl.BlockSpec(memory_space=pl.ANY)
    dma = pltpu.SemaphoreType.DMA
    return pl.pallas_call(
        kernel,
        out_shape=pltpu.VMEM((ROWS, 512), BF),
        in_specs=[anyspec] * 6 + [pl.BlockSpec(memory_space=pltpu.SMEM), anyspec],
        out_specs=pl.BlockSpec(memory_space=pltpu.VMEM),
        scratch_shapes=[
            pltpu.VMEM((16, ROWS, CH), BF),
            pltpu.VMEM((4, WIDTH, 256), BF),
            pltpu.VMEM((2048, 512), BF),
            pltpu.VMEM((2, HD, HD), F32),
            pltpu.VMEM((4, ROWS, 256), F32),
            pltpu.VMEM((ROWS, HD), F32),
            pltpu.VMEM((2, HD, ROWS), F32),
            pltpu.VMEM((2, ROWS, HD), F32),
            pltpu.VMEM((2, ROWS, HD), F32),
            pltpu.VMEM((ROWS, 256), BF),
            pltpu.VMEM((ROWS, 256), BF),
            pltpu.VMEM((ROWS, 256), BF),
            pltpu.VMEM((ROWS, 256), F32),
            pltpu.VMEM((ROWS, 256), F32),
            pltpu.VMEM((NZ, 32, HD), BF),
            pltpu.VMEM((NZ, 32, HD), BF),
            pltpu.VMEM((32, HD), F32),
            pltpu.VMEM((NY, 32, HD), F32),
            pltpu.VMEM((NZ, 32, HD), BF),
            pltpu.VMEM((NZ, 32, HD), BF),
            pltpu.VMEM((8, ROWS, 256), BF),
            pltpu.VMEM((ROWS, 512), F32),
            dma((8,)), dma((28,)), dma((32,)), dma((7,)), dma((8,)), dma((3,)), dma((4,)),
            dma((7,)), dma((8,)), dma((28,)), dma((32,)),
            pltpu.SemaphoreType.REGULAR((10,)),
        ],
        compiler_params=pltpu.CompilerParams(
            collective_id=0, has_side_effects=True, vmem_limit_bytes=56 * 1024 * 1024),
        name="lightning_layer",
    )(tokens, w_query, w_key, w_value, w_gate, w_out, decay_rate, state_in)


def solution(mesh):
    return jax.shard_map(
        per_device,
        mesh=mesh,
        in_specs=(
            P("seq", "tp"),
            P(None, "tp"),
            P(None, "tp"),
            P(None, "tp"),
            P(None, "tp"),
            P(None, "tp"),
            P(),
            P("tp", None, None),
        ),
        out_specs=P("seq", "tp"),
        check_vma=False,
    )
```

```python
import jax
import jax.numpy as jnp
from jax import lax
from jax.experimental import pallas as pl
from jax.experimental.pallas import tpu as pltpu
from jax.sharding import PartitionSpec as P

NX, NY, NZ = 4, 4, 8
ROWS = 512
WIDTH = 4096
HD = 128
CH = 256
BF = jnp.bfloat16
F32 = jnp.float32


def silu(z):
    return z / (1.0 + jnp.exp(-z))


def kernel(tok_in, wq, wk, wv, wg, wo, rate_ref, st_in, out_ref,
           tok, w, wov, stv, acc, sq, mask, tail, lead, kb, vb, qb, gate, intra,
           lsend, r1, rtsend, rt, ssend, srecv, hid, oacc,
           load_sem, tok_send, tok_recv, s1s, s1r, s2s, s2r, s3s, s3r, hid_send, hid_recv, here):
    tp = lax.axis_index("tp")
    seq = lax.axis_index("seq")
    x, core = tp // 2, tp % 2
    y, z = seq // NZ, seq % NZ
    xr, xl, xo = (x + 1) % NX, (x + 3) % NX, (x + 2) % NX
    right, left = (seq, 2 * xr + core), (seq, 2 * xl + core)
    partner = (seq, 2 * x + 1 - core)
    mine, other = core, 1 - core

    def signal(dev):
        pl.semaphore_signal(barrier, inc=1, device_id=dev, device_id_type=pl.DeviceIdType.MESH)

    def remote(src, dst, ss, rs, dev):
        return pltpu.make_async_remote_copy(
            src_ref=src, dst_ref=dst, send_sem=ss, recv_sem=rs, device_id=dev,
            device_id_type=pl.DeviceIdType.MESH)

    loads = []
    for f in range(2):
        loads.append(pltpu.make_async_copy(
            tok_in.at[:, pl.ds(f * CH, CH)], tok.at[2 * tp + f], load_sem.at[f]))
    for j, ref in enumerate((wq, wk, wv, wg)):
        loads.append(pltpu.make_async_copy(ref, w.at[j], load_sem.at[2 + j]))
    loads.append(pltpu.make_async_copy(wo, wov, load_sem.at[6]))
    loads.append(pltpu.make_async_copy(st_in, stv, load_sem.at[7]))
    for c in loads:
        c.start()

    barrier = pltpu.get_barrier_semaphore()
    z_up, z_down = (y * NZ + (z + 1) % NZ, tp), (y * NZ + (z + NZ - 1) % NZ, tp)
    y_up, y_down = (((y + 1) % NY) * NZ + z, tp), (((y + NY - 1) % NY) * NZ + z, tp)
    for dev in (right, left, partner, z_up, z_down, y_up, y_down):
        signal(dev)
    pl.semaphore_wait(barrier, 7)

    def greet(n):
        for k, dev in enumerate((z_up, z_down) + ((y_up, y_down) if n == 0 else ())):
            pl.semaphore_signal(here.at[4 * n + k], inc=1, device_id=dev,
                                device_id_type=pl.DeviceIdType.MESH)

    def greeted(n):
        for k in range(4 if n == 0 else 2):
            pl.semaphore_wait(here.at[4 * n + k], 1)

    greet(0)
    sends = []

    def go(copy):
        copy.start()
        sends.append(copy)

    HALF = ROWS // 2

    def tok_copy(n, slot, half, dev):
        ref = tok.at[slot, pl.ds(half * HALF, HALF)]
        return remote(ref, ref, tok_send.at[n], tok_recv.at[2 * slot + half], dev)

    def tok_go(slot, half, dev):
        go(tok_copy(len(sends), slot, half, dev))

    def tok_wait(slot):
        for half in range(2):
            tok_copy(0, slot, half, partner).wait_recv()

    def slot(xx, cc, f):
        return (2 * xx + cc) * 2 + f

    loads[0].wait()
    for half in range(2):
        tok_go(slot(x, mine, 0), half, right)
    loads[1].wait()
    for half in range(2):
        tok_go(slot(x, mine, 1), half, left)
    for f in range(2):
        for half in range(2):
            tok_go(slot(x, mine, f), half, partner)
    for half in range(2):
        tok_go(slot(x, mine, 1), half, right)
        tok_go(slot(x, mine, 0), half, left)

    rates = [rate_ref[2 * tp + h] for h in range(2)]
    pos = lax.broadcasted_iota(jnp.int32, (ROWS, HD), 0).astype(F32)
    gap = (lax.broadcasted_iota(jnp.int32, (HD, ROWS), 0) + (ROWS - HD)
           - lax.broadcasted_iota(jnp.int32, (HD, ROWS), 1))
    lower = gap >= 0
    gap_f = jnp.where(lower, gap, 0).astype(F32)
    for h in range(2):
        tail[h] = jnp.exp(-rates[h] * (ROWS - 1.0 - pos))
        lead[h] = jnp.exp(-rates[h] * (pos + 1.0))
        mask[h] = jnp.where(lower, jnp.exp(-rates[h] * gap_f), 0.0)

    def project(s1, s2, first=False, lo=0, hi=4, squares=True):
        rows1 = pl.ds(pl.multiple_of(s1 * CH, CH), CH)
        rows2 = pl.ds(pl.multiple_of(s2 * CH, CH), CH)

        def body(j, carry):
            part = jnp.dot(tok[s1], w[j, rows1, :], preferred_element_type=F32)
            part += jnp.dot(tok[s2], w[j, rows2, :], preferred_element_type=F32)
            if first:
                acc[j] = part
            else:
                acc[j] += part
            return carry

        lax.fori_loop(lo, hi, body, 0)
        if not squares:
            return
        a = tok[s1].astype(F32)
        b = tok[s2].astype(F32)
        a = a * a
        b = b * b
        total = (a[:, :HD] + a[:, HD:]) + (b[:, :HD] + b[:, HD:])
        if first:
            sq[...] = total
        else:
            sq[...] += total

    def pass_on(s_left, s_right, forward):
        for half in range(2):
            tok_copy(0, s_left, half, partner).wait_recv()
            if forward:
                tok_go(s_left, half, right)
            tok_go(s_left, half, partner)
            tok_copy(0, s_right, half, partner).wait_recv()
            if forward:
                tok_go(s_right, half, left)
            tok_go(s_right, half, partner)

    for c in loads[2:6]:
        c.wait()
    project(slot(x, mine, 0), slot(x, mine, 1), True)
    greeted(0)
    greet(1)
    tok_wait(slot(x, other, 0))
    tok_wait(slot(x, other, 1))
    project(slot(x, other, 0), slot(x, other, 1))

    pass_on(slot(xl, mine, 0), slot(xr, mine, 1), True)
    project(slot(xl, mine, 0), slot(xr, mine, 1))
    greeted(1)
    greet(2)
    tok_wait(slot(xl, other, 0))
    tok_wait(slot(xr, other, 1))
    project(slot(xl, other, 0), slot(xr, other, 1))

    pass_on(slot(xl, mine, 1), slot(xr, mine, 0), False)
    project(slot(xl, mine, 1), slot(xr, mine, 0))
    tok_wait(slot(xl, other, 1))
    tok_wait(slot(xr, other, 0))
    project(slot(xl, other, 1), slot(xr, other, 0))

    pass_on(slot(xo, mine, 0), slot(xo, mine, 1), False)
    project(slot(xo, mine, 0), slot(xo, mine, 1))
    tok_wait(slot(xo, other, 0))
    tok_wait(slot(xo, other, 1))
    last = (slot(xo, other, 0), slot(xo, other, 1))
    project(*last, lo=1, hi=3)
    greeted(2)

    inv = lax.rsqrt(jnp.sum(sq[...], axis=1, keepdims=True) / float(WIDTH) + 1e-06)
    kb[...] = silu(acc[1] * inv).astype(BF)
    vb[...] = (acc[2] * inv).astype(BF)

    for h in range(2):
        cols = slice(h * HD, (h + 1) * HD)
        scaled = (kb[:, cols].astype(F32) * tail[h]).astype(BF)
        state = lax.dot_general(scaled, vb[:, cols], (((0,), (0,)), ((), ())),
                                preferred_element_type=F32)
        lsend[h * 4:(h + 1) * 4] = state.astype(BF).reshape(4, 32, HD)

    far_first = (4, 3, 5, 2, 6, 1, 7)
    for n, d in enumerate(far_first):
        zz = (z + d) % NZ
        go(remote(lsend.at[zz], r1.at[z], s1s.at[n], s1r.at[z], (y * NZ + zz, tp)))
    r1[z] = lsend[z]

    project(*last, lo=0, hi=1, squares=False)
    qb[...] = silu(acc[0] * inv).astype(BF)

    def attend(h):
        cols = slice(h * HD, (h + 1) * HD)
        for i in range(4):
            n = (i + 1) * HD
            rows = slice(i * HD, n)
            scores = lax.dot_general(qb[rows, cols], kb[0:n, cols], (((1,), (1,)), ((), ())),
                                     preferred_element_type=F32)
            weights = (scores * mask[h, :, ROWS - n:]).astype(BF)
            intra[rows, cols] = jnp.dot(weights, vb[0:n, cols], preferred_element_type=F32)

    attend(0)
    for d in far_first[::-1]:
        zz = (z + d) % NZ
        remote(lsend.at[zz], r1.at[zz], s1s.at[0], s1r.at[zz], partner).wait_recv()
    rate_z = rate_ref[2 * tp + z // 4]
    step = jnp.exp(jnp.full((1, HD), -rate_z * ROWS, F32))
    run = jnp.zeros((32, HD), F32)
    before = []
    for k in range(NZ):
        before.append(run)
        run = step * run + r1[k].astype(F32)
    rtsend[...] = run
    for n, d in enumerate((2, 1, 3)):
        yy = (y + d) % NY
        go(remote(rtsend, rt.at[y], s2s.at[n], s2r.at[y], (yy * NZ + z, tp)))
    rt[y] = run
    for d in (1, 3, 2):
        yy = (y + d) % NY
        remote(rtsend, rt.at[yy], s2s.at[0], s2r.at[yy], partner).wait_recv()
    start = jnp.zeros((32, HD), F32)
    for k in range(NY):
        gone = jnp.maximum(y - 1 - k, 0).astype(F32) * float(NZ * ROWS)
        factor = jnp.exp(jnp.full((1, HD), -rate_z * gone, F32))
        start += jnp.where(k < y, factor, 0.0) * rt[k]
    for k in range(NZ):
        factor = jnp.exp(jnp.full((1, HD), -rate_z * float(k * ROWS), F32))
        ssend[k] = (before[k] + factor * start).astype(BF)
    for n, d in enumerate(far_first):
        zz = (z + d) % NZ
        go(remote(ssend.at[zz], srecv.at[z], s3s.at[n], s3r.at[z], (y * NZ + zz, tp)))
    srecv[z] = ssend[z]
    project(*last, lo=3, hi=4, squares=False)
    attend(1)
    gate[...] = silu(acc[3] * inv)
    loads[6].wait()
    loads[7].wait()
    for d in far_first[::-1]:
        zz = (z + d) % NZ
        remote(ssend.at[zz], srecv.at[zz], s3s.at[0], s3r.at[zz], partner).wait_recv()
    parts = []
    offset = (ROWS * seq).astype(F32)
    for h in range(2):
        incoming = srecv[h * 4:(h + 1) * 4].astype(F32).reshape(HD, HD)
        incoming += jnp.exp(jnp.full((1, HD), -rates[h] * offset, F32)) * stv[h]
        high = incoming.astype(BF)
        parts.append((high, (incoming - high.astype(F32)).astype(BF)))

    QUARTER = ROWS // 4
    first_hid = len(sends)

    def hid_copy(n, sl, part, dev):
        ref = hid.at[sl, pl.ds(part * QUARTER, QUARTER)]
        return remote(ref, ref, hid_send.at[n], hid_recv.at[4 * sl + part], dev)

    def hid_go(sl, part, *devs):
        for dev in devs:
            go(hid_copy(len(sends) - first_hid, sl, part, dev))

    def hid_wait(sl, part):
        hid_copy(0, sl, part, partner).wait_recv()

    for part in (0, 2, 1, 3):
        rows = slice(part * QUARTER, (part + 1) * QUARTER)
        for h in range(2):
            cols = slice(h * HD, (h + 1) * HD)
            q = qb[rows, cols]
            inter = jnp.dot(q, parts[h][0], preferred_element_type=F32)
            inter += jnp.dot(q, parts[h][1], preferred_element_type=F32)
            att = intra[rows, cols] + lead[h, rows, :] * inter
            norm = lax.rsqrt(jnp.mean(att * att, axis=1, keepdims=True) + 1e-06)
            hid[tp, rows, cols] = (att * norm * gate[rows, cols]).astype(BF)
        hid_go(tp, part, right if part < 2 else left, partner)
    for i in range(2):
        hid_go(tp, 2 + i, right)
        hid_go(tp, i, left)

    def out_part(sl, half, first=False):
        rows = slice(half * HALF, (half + 1) * HALF)
        part = jnp.dot(hid[sl, rows, :], wov[pl.ds(pl.multiple_of(sl * CH, CH), CH), :],
                       preferred_element_type=F32)
        if first:
            oacc[rows, :] = part
        else:
            oacc[rows, :] += part

    def arrived(sl, half):
        hid_wait(sl, 2 * half)
        hid_wait(sl, 2 * half + 1)
        out_part(sl, half)

    tl, tr, to = 2 * xl, 2 * xr, 2 * xo
    tpp = 2 * x + other
    out_part(tp, 0, True)
    out_part(tp, 1, True)
    arrived(tpp, 0)
    arrived(tpp, 1)

    for i in range(2):
        hid_wait(tl + mine, i)
        hid_go(tl + mine, i, right, partner)
        hid_wait(tr + mine, 2 + i)
        hid_go(tr + mine, 2 + i, left, partner)
    out_part(tl + mine, 0)
    out_part(tr + mine, 1)
    arrived(tl + other, 0)
    arrived(tr + other, 1)

    for i in range(2):
        hid_wait(tl + mine, 2 + i)
        hid_go(tl + mine, 2 + i, partner)
        hid_wait(tr + mine, i)
        hid_go(tr + mine, i, partner)
    out_part(tl + mine, 1)
    out_part(tr + mine, 0)
    arrived(tl + other, 1)
    arrived(tr + other, 0)

    for i in range(2):
        hid_wait(to + mine, i)
        hid_go(to + mine, i, partner)
        hid_wait(to + mine, 2 + i)
        hid_go(to + mine, 2 + i, partner)
    out_part(to + mine, 0)
    out_part(to + mine, 1)
    arrived(to + other, 0)
    arrived(to + other, 1)

    for f in range(2):
        cols = slice(f * CH, (f + 1) * CH)
        out_ref[:, cols] = (tok[2 * tp + f].astype(F32) + oacc[:, cols]).astype(BF)
    for c in sends:
        c.wait_send()


def per_device(tokens, w_query, w_key, w_value, w_gate, w_out, decay_rate, state_in):
    anyspec = pl.BlockSpec(memory_space=pl.ANY)
    dma = pltpu.SemaphoreType.DMA
    return pl.pallas_call(
        kernel,
        out_shape=pltpu.VMEM((ROWS, 512), BF),
        in_specs=[anyspec] * 6 + [pl.BlockSpec(memory_space=pltpu.SMEM), anyspec],
        out_specs=pl.BlockSpec(memory_space=pltpu.VMEM),
        scratch_shapes=[
            pltpu.VMEM((16, ROWS, CH), BF),
            pltpu.VMEM((4, WIDTH, 256), BF),
            pltpu.VMEM((2048, 512), BF),
            pltpu.VMEM((2, HD, HD), F32),
            pltpu.VMEM((4, ROWS, 256), F32),
            pltpu.VMEM((ROWS, HD), F32),
            pltpu.VMEM((2, HD, ROWS), F32),
            pltpu.VMEM((2, ROWS, HD), F32),
            pltpu.VMEM((2, ROWS, HD), F32),
            pltpu.VMEM((ROWS, 256), BF),
            pltpu.VMEM((ROWS, 256), BF),
            pltpu.VMEM((ROWS, 256), BF),
            pltpu.VMEM((ROWS, 256), F32),
            pltpu.VMEM((ROWS, 256), F32),
            pltpu.VMEM((NZ, 32, HD), BF),
            pltpu.VMEM((NZ, 32, HD), BF),
            pltpu.VMEM((32, HD), F32),
            pltpu.VMEM((NY, 32, HD), F32),
            pltpu.VMEM((NZ, 32, HD), BF),
            pltpu.VMEM((NZ, 32, HD), BF),
            pltpu.VMEM((8, ROWS, 256), BF),
            pltpu.VMEM((ROWS, 512), F32),
            dma((8,)), dma((28,)), dma((32,)), dma((7,)), dma((8,)), dma((3,)), dma((4,)),
            dma((7,)), dma((8,)), dma((28,)), dma((32,)),
            pltpu.SemaphoreType.REGULAR((10,)),
        ],
        compiler_params=pltpu.CompilerParams(
            collective_id=0, has_side_effects=True, vmem_limit_bytes=56 * 1024 * 1024),
        name="lightning_layer",
    )(tokens, w_query, w_key, w_value, w_gate, w_out, decay_rate, state_in)


def solution(mesh):
    return jax.shard_map(
        per_device,
        mesh=mesh,
        in_specs=(
            P("seq", "tp"),
            P(None, "tp"),
            P(None, "tp"),
            P(None, "tp"),
            P(None, "tp"),
            P(None, "tp"),
            P(),
            P("tp", None, None),
        ),
        out_specs=P("seq", "tp"),
        check_vma=False,
    )
```
